256 devices in a mesh: param: 16 (over z, core), ex: 16 (over x, y).
Axes of the slice: x: 4, y: 4, z: 8, core: 2. Of those that a mesh axis runs over, the one named last changes fastest.
Arguments:
- query_acts: bfloat16 [16, 256, 16, 4096], P(None, 'ex', None, 'param'), may hold values from -6 to 6
- query_grads: bfloat16 [16, 256, 16, 4096], P(None, 'ex', None, 'param'), may hold values from -6 to 6
- train_acts: bfloat16 [16, 512, 16, 4096], P(None, 'ex', None, 'param'), as said below
- train_grads: bfloat16 [16, 512, 16, 4096], P(None, 'ex', None, 'param'), as said below
- input_projection: bfloat16 [4096, 128], P('param'), as said below
- proj_out: bfloat16 [4096, 64], P('param'), as said below
- query_clusters: int32 [16, 256], P('param'), may hold values from 0 to 127
- train_clusters: int32 [16, 512], P(None, 'ex'), may hold values from 0 to 127
- pair_mask: int32 [128, 128], replicated, may hold values 0 or 1
Outputs:
- scores: float32 [16, 256, 16, 512], P('param', None, None, 'ex')
- cluster_scores: float32 [16, 256, 128], P('param', 'ex')
The draws below stay inside these ranges and needn't reach their ends.
Inputs may be any that keep to these rules, and one draw needn't show every extreme that they name: `train_acts`: token features whose scales differ from token to token and from example to example. `train_grads`: token gradients whose scales differ from example to example. `input_projection`: random projection columns of differing scales. `proj_out`: random projection columns of differing scales.
All inputs are finite; a program needn't handle non-finite values.
Results may differ from the reference program's by a relative error of at most 0.022.
The reference program's roundings to bfloat16 on the way count: a program that leaves them out, or rounds other values in their place, can miss the bound.
Values may be sent and summed in bfloat16 or wider, within the bound.
A program may use at most 128 MiB of HBM per device.

```python
import math
import jax
import jax.numpy as jnp
from jax import lax

D = 4096
R_IN = 128
R_OUT = 64
K = 16
NC = 128
GROUPS = 16
NQ_G = 256
NT_G = 512
NT = 8192
DIMS = 8192


def token_base(key, shape):
    return jax.random.normal(key, shape, jnp.float32)


def draw_train_acts(key, part):
    first, second = jax.random.split(key, 2)
    base = token_base(first, (GROUPS, NT_G, K, D))
    rank = jnp.arange(NT_G, dtype=jnp.float32) / NT_G
    rise = 1.0 + 2.0 * rank
    spread = jnp.exp(jax.random.uniform(second, (GROUPS, NT_G, K, 1), jnp.float32, 0.0, math.log(10.0)))
    return (0.3 * base * rise[None, :, None, None] * spread).astype(jnp.bfloat16)


def draw_train_grads(key, part):
    first, second = jax.random.split(key)
    base = token_base(first, (GROUPS, NT_G, K, D))
    rank = jnp.arange(GROUPS, dtype=jnp.float32) / GROUPS
    rise = 1.0 + 2.0 * rank
    spread = jnp.exp(jax.random.uniform(second, (GROUPS, NT_G, 1, 1), jnp.float32, 0.0, math.log(4.0)))
    return (0.5 * base * rise[:, None, None, None] * spread).astype(jnp.bfloat16)


def projection(key, width):
    first, second, third, fourth = jax.random.split(key, 4)
    base = token_base(first, (D, width))
    column = jnp.exp(jax.random.uniform(second, (1, width), jnp.float32, math.log(0.3), math.log(3.0)))
    shared = jax.random.normal(third, (D, 1), jnp.float32) * jax.random.normal(fourth, (1, width), jnp.float32) * 0.7
    return ((base * column + shared) * D ** (-0.5)).astype(jnp.bfloat16)


def draw_input_projection(key, part):
    return projection(key, R_IN)


def draw_proj_out(key, part):
    return projection(key, R_OUT)


def touch_ends(entries, rng, smallest, top_value):
    dims = entries.shape
    index_at = [jax.random.randint(jax.random.fold_in(rng, axis), (), 0, dims[axis]) for axis in range(len(dims))]
    entries = entries.at[tuple(index_at)].set(smallest)
    longest = dims.index(max(dims))
    index_at[longest] = (index_at[longest] + 1) % dims[longest]
    return entries.at[tuple(index_at)].set(top_value)


def levels(key, shape, cuts, smallest, largest):
    level, own = 1.0, jax.random.fold_in(key, 6)
    for axis_at, shards_of in cuts:
        steps = jnp.exp(jax.random.uniform(jax.random.fold_in(own, axis_at), (shards_of,), jnp.float32, smallest / len(cuts), largest / len(cuts)))
        level = level * jnp.repeat(steps, shape[axis_at] // shards_of).reshape([-1 if axis == axis_at else 1 for axis in range(len(shape))])
    return level


def noise(key, extent, deviation, reach, cuts=(), kind=jnp.bfloat16):
    factor_of = levels(key, extent, cuts, -0.22, 0.18) if cuts else 1.0
    values = jax.random.normal(key, extent, jnp.float32) * deviation * factor_of
    return jnp.minimum(jnp.maximum(values, -reach), reach).astype(kind)


def setup_inputs(seed: int = 0) -> dict:
    splits = jax.random.split(jax.random.key(seed), 10)
    return {
        "query_acts": noise(splits[0], (GROUPS, NQ_G, K, D), 1.0, 6.0, ((1, 16), (3, 16))),
        "query_grads": noise(splits[1], (GROUPS, NQ_G, K, D), 1.0, 6.0, ((1, 16), (3, 16))),
        "train_acts": draw_train_acts(jax.random.fold_in(splits[9], 71), 0),
        "train_grads": draw_train_grads(jax.random.fold_in(splits[9], 71), 0),
        "input_projection": draw_input_projection(jax.random.fold_in(splits[9], 71), 0),
        "proj_out": draw_proj_out(jax.random.fold_in(splits[9], 71), 0),
        "query_clusters": touch_ends(jax.random.randint(splits[6], (GROUPS, NQ_G), 0, NC), jax.random.fold_in(splits[6], 1), 0, NC - 1).astype(jnp.int32),
        "train_clusters": touch_ends(jax.random.randint(splits[7], (GROUPS, NT_G), 0, NC), jax.random.fold_in(splits[7], 1), 0, NC - 1).astype(jnp.int32),
        "pair_mask": touch_ends((jax.random.randint(splits[8], (NC, NC), 0, 2) < 1).astype(jnp.int32), jax.random.fold_in(splits[8], 1), 0, 1),
    }


def inverse_of(gram, count):
    mean = gram / count
    size = gram.shape[0]
    damping = 0.1 * jnp.trace(mean) / size
    identity = jnp.eye(size, dtype=gram.dtype)
    factor = jnp.linalg.cholesky(mean + damping * identity)
    return jax.scipy.linalg.cho_solve((factor, True), identity)

def reference(query_acts, query_grads, train_acts, train_grads, input_projection, proj_out, query_clusters, train_clusters, pair_mask):

    def project(pair):
        acts, grads = pair
        lead = acts.shape[:2]
        part_in = jnp.dot(acts.reshape(-1, D).astype(jnp.float32), input_projection.astype(jnp.float32), preferred_element_type=jnp.float32)
        part_out = jnp.dot(grads.reshape(-1, D).astype(jnp.float32), proj_out.astype(jnp.float32), preferred_element_type=jnp.float32)
        return (part_in.astype(jnp.bfloat16).reshape(lead + (R_IN,)), part_out.astype(jnp.bfloat16).reshape(lead + (R_OUT,)))
    query_in, query_output_side = lax.map(project, (query_acts, query_grads))
    train_in, train_out = lax.map(project, (train_acts, train_grads))
    flat_in = train_in.reshape(-1, R_IN)
    flat_out = train_out.reshape(-1, R_OUT)
    gram_in = jnp.dot(flat_in.T.astype(jnp.float32), flat_in.astype(jnp.float32), preferred_element_type=jnp.float32)
    gram_out = jnp.dot(flat_out.T.astype(jnp.float32), flat_out.astype(jnp.float32), preferred_element_type=jnp.float32)
    count = float(NT * K)
    inv_in = inverse_of(gram_in, count)
    inv_out = inverse_of(gram_out, count)
    preconditioned_input = jnp.dot(query_in.reshape(-1, R_IN).astype(jnp.float32), inv_in, precision=lax.Precision.HIGHEST).reshape(GROUPS, NQ_G, K, R_IN)
    preconditioned_output = jnp.dot(query_output_side.reshape(-1, R_OUT).astype(jnp.float32), inv_out, precision=lax.Precision.HIGHEST).reshape(GROUPS, NQ_G, K, R_OUT)
    query_before_preconditioning = jnp.einsum('gqkr,gqks->gqrs', preconditioned_output, preconditioned_input, precision=lax.Precision.HIGHEST)
    query_before_preconditioning = query_before_preconditioning.reshape(GROUPS, NQ_G, DIMS).astype(jnp.bfloat16)

    def form(pair):
        part_out, part_in = pair
        grad = jnp.einsum('tkr,tks->trs', part_out.astype(jnp.float32), part_in.astype(jnp.float32), precision=lax.Precision.HIGHEST)
        return grad.reshape(NT_G, DIMS).astype(jnp.bfloat16)
    train_grad = lax.map(form, (train_out, train_in)).reshape(NT, DIMS)
    train_ids = train_clusters.reshape(-1)
    onehot = (train_ids[:, None] == jnp.arange(NC, dtype=jnp.int32)[None, :]).astype(jnp.float32)
    scale = 1.0 / (K * math.sqrt(DIMS))
    factor = math.sqrt(NC / NT)

    def score_group(pair):
        rows, ids = pair
        raw = jnp.dot(rows.astype(jnp.float32), train_grad.T.astype(jnp.float32), preferred_element_type=jnp.float32)
        allowed = pair_mask[ids][:, train_ids].astype(jnp.float32)
        block = raw * scale * allowed
        sums = jnp.dot(block, onehot, precision=lax.Precision.HIGHEST) * factor
        return (block.reshape(NQ_G, GROUPS, NT_G), sums)
    scores, cluster_scores = lax.map(score_group, (query_before_preconditioning, query_clusters))
    return (scores, cluster_scores)
```

```python
import functools
import math

import jax
import jax.numpy as jnp
from jax import lax
from jax.experimental import pallas as pl
from jax.experimental.pallas import tpu as pltpu
from jax.sharding import PartitionSpec as P

MESH = pl.DeviceIdType.MESH
F32 = jnp.float32
BF16 = jnp.bfloat16
NT = (((1,), (1,)), ((), ()))
TN = (((0,), (0,)), ((), ()))

T_IN, T_ALL = 512, 768
Q_IN, ALL = 256, 1152
Q_ALL = ALL - T_ALL


def remote(src, dst, send, recv, device):
    return pltpu.make_async_remote_copy(
        src_ref=src, dst_ref=dst, send_sem=send, recv_sem=recv, device_id=device, device_id_type=MESH
    )


def spot(p, e):
    return {"param": p, "ex": e}


def halves(chunk):
    size = (T_ALL, Q_ALL)[chunk] // 2
    return (pl.ds(0, size), pl.ds(size, size))


def reduce_kernel(
    nz,
    qa, qg, ta, tg, win, wout,
    out,
    qa_b, qg_b, ta_b, tg_b, part_t, part_q, sib_t, sib_q, snd_t, snd_q, rcv_t, rcv_q,
    in_sem, sib_send, sib_recv, ring_send, ring_recv,
):
    p, e = lax.axis_index("param"), lax.axis_index("ex")
    z, c = p // 2, p % 2
    sibling = spot(z * 2 + 1 - c, e)
    ring = (spot(lax.rem(z + 1, nz) * 2 + c, e), spot(lax.rem(z + nz - 1, nz) * 2 + c, e))
    far = nz // 2

    def shift(k):
        m = far - (k + 1) // 2
        return jnp.where(k % 2 == 1, m, nz - m) % nz

    def group(u):
        k = u // 2
        core = jnp.where(u % 2 == 0, 1 - c, c)
        return lax.rem(z + shift(k), nz) * 2 + core

    pairs = ((ta, ta_b), (tg, tg_b), (qa, qa_b), (qg, qg_b))

    def loads(u):
        g = group(u)
        return [
            pltpu.make_async_copy(src.at[g], dst.at[u], in_sem.at[i, u])
            for i, (src, dst) in enumerate(pairs)
        ]

    def start(u, carry):
        for copy in loads(u):
            copy.start()
        return carry

    lax.fori_loop(0, 2 * nz, start, 0)
    barrier = pltpu.get_barrier_semaphore()
    for device in (sibling,) + ring:
        pl.semaphore_signal(barrier, inc=1, device_id=device, device_id_type=MESH)
    pl.semaphore_wait(barrier, 3)

    w_in = win[...]
    narrow = wout[...].astype(F32).T
    blank = jnp.zeros_like(narrow)
    w_low = jnp.concatenate([narrow, blank], axis=1).astype(BF16)
    w_high = jnp.concatenate([blank, narrow], axis=1).astype(BF16)

    def dot(a, b):
        return jnp.dot(a, b, preferred_element_type=F32)

    parts, sibs, sends, recvs = (part_t, part_q), (sib_t, sib_q), (snd_t, snd_q), (rcv_t, rcv_q)

    def to_sibling(k, chunk):
        return remote(
            parts[chunk].at[0, k], sibs[chunk].at[k], sib_send.at[chunk, k], sib_recv.at[chunk, k], sibling
        )

    def project(u, carry):
        for copy in loads(u):
            copy.wait()
        k, own = u // 2, u % 2
        part_t[own, k, 0:T_IN, :] = dot(ta_b[u], w_in).astype(BF16)
        part_t[own, k, T_IN:T_ALL, :] = (
            dot(tg_b[u, 0:256, :], w_low) + dot(tg_b[u, 256:512, :], w_high)
        ).astype(BF16)

        @pl.when(own == 0)
        def _():
            to_sibling(k, 0).start()

        part_q[own, k, 0:Q_IN, :] = dot(qa_b[u], w_in)
        part_q[own, k, Q_IN:Q_ALL, :] = dot(qg_b[u, 0:128, :], w_low) + dot(qg_b[u, 128:256, :], w_high)

        @pl.when(own == 0)
        def _():
            to_sibling(k, 1).start()

        return carry

    def hop(way, step, chunk, half):
        rows = halves(chunk)[half]
        return remote(
            sends[chunk].at[way, step, rows],
            recvs[chunk].at[way, step, rows],
            ring_send.at[way, step, chunk, half],
            ring_recv.at[way, step, chunk, half],
            ring[way],
        )

    def own_sum(k, chunk, rows):
        return parts[chunk][1, k, rows, :].astype(F32) + sibs[chunk][k, rows, :].astype(F32)

    hops = []

    def send(way, step, chunk, half):
        rows = halves(chunk)[half]
        k = 0 if step == 0 else 2 * step - 1 + way
        value = own_sum(k, chunk, rows)
        if step >= 2 or (step == 1 and half == way):
            hop(way, step - 1, chunk, half).wait_recv()
            value = value + recvs[chunk][way, step - 1, rows, :].astype(F32)
        sends[chunk][way, step, rows, :] = value.astype(sends[chunk].dtype)
        copy = hop(way, step, chunk, half)
        copy.start()
        hops.append(copy)

    def round_of(step, chunk):
        if step == 0:
            for way in (0, 1):
                send(way, 0, chunk, way)
            return
        for late in (1, 0):
            for way in (0, 1):
                send(way, step, chunk, way if late == 0 else 1 - way)

    for step in range(far):
        low, high = (0, 2) if step == 0 else (4 * step - 2, 4 * step + 2)
        lax.fori_loop(low, high, project, 0)
        for k in range(low // 2, high // 2):
            to_sibling(k, 0).wait_recv()
            to_sibling(k, 1).wait_recv()
        round_of(step, 0)
    round_of(0, 1)
    lax.fori_loop(2 * nz - 2, 2 * nz, project, 0)
    to_sibling(nz - 1, 0).wait_recv()
    to_sibling(nz - 1, 1).wait_recv()

    def final(chunk):
        for half in (1, 0):
            rows = halves(chunk)[half]
            value = own_sum(nz - 1, chunk, rows)
            for way in (0, 1):
                hop(way, far - 1, chunk, half).wait_recv()
                value = value + recvs[chunk][way, far - 1, rows, :].astype(F32)
            out[pl.ds(T_ALL * chunk + rows.start, rows.size), :] = value.astype(BF16)

    for step in range(1, far):
        round_of(step, 1)
    final(0)
    final(1)
    for copy in hops:
        copy.wait_send()
    for k in range(nz):
        to_sibling(k, 0).wait_send()
        to_sibling(k, 1).wait_send()


def newton(damped, level, steps, scalings):
    size = damped.shape[0]
    rows = lax.broadcasted_iota(jnp.int32, (size, size), 0)
    eye = (rows == lax.broadcasted_iota(jnp.int32, (size, size), 1)).astype(F32)

    def dot(a, b):
        return jnp.dot(a, b, preferred_element_type=F32, precision=lax.Precision.HIGHEST)

    resid = eye - level * damped
    guess = level * eye
    for index in range(steps):
        c = scalings[index]
        grown = guess + (level * resid if index == 0 else dot(guess, resid))
        resid = (1.0 - c) * eye + c * dot(resid, resid)
        guess = c * grown
    for _ in range(2):
        resid = eye - dot(damped, guess)
        guess = guess + dot(guess, resid)
    return 0.5 * (guess + guess.T)


def schedule_of(size):
    kappa = 1.0 + 10.0 * size
    rho = (kappa - 1.0) / (kappa + 1.0)
    scalings = []
    while rho > 1e-4:
        scalings.append(2.0 / (2.0 - rho * rho))
        rho = rho * rho / (2.0 - rho * rho)
    return 2.0 / (1.0 + kappa), scalings


def inverse_of(gram, count):
    size = gram.shape[0]
    mean = gram * (1.0 / count)
    rows = lax.broadcasted_iota(jnp.int32, (size, size), 0)
    diagonal = rows == lax.broadcasted_iota(jnp.int32, (size, size), 1)
    floor = 0.1 / size * jnp.sum(jnp.where(diagonal, mean, 0.0), keepdims=True)
    damped = mean + jnp.where(diagonal, floor, 0.0)
    level, scalings = schedule_of(size)
    return newton(damped, level / floor, len(scalings), scalings)


def score_kernel(
    nz, ne, count, scale, spread,
    fac, query_ids, train_ids, mask,
    scores, sums,
    tf, qf, gl, g1, g2, g3, s1, s2, tmat, qmat, ot, raw, allow, cs, cr,
    g_send, g_recv, q_send, q_recv, t_send, t_recv, sib_send, sib_recv, c_send, c_recv,
):
    p, e = lax.axis_index("param"), lax.axis_index("ex")
    np_ = 2 * nz
    z, c = p // 2, p % 2
    sibling = spot(z * 2 + 1 - c, e)
    ring = (spot(lax.rem(z + 1, nz) * 2 + c, e), spot(lax.rem(z + nz - 1, nz) * 2 + c, e))
    far = nz // 2

    barrier = pltpu.get_barrier_semaphore()

    def greet(o, carry):
        pl.semaphore_signal(barrier, inc=1, device_id=spot(p, lax.rem(e + o, ne)), device_id_type=MESH)
        return carry

    def greet_column(o, carry):
        pl.semaphore_signal(barrier, inc=1, device_id=spot(lax.rem(p + o, np_), e), device_id_type=MESH)
        return carry

    lax.fori_loop(1, ne, greet, 0)
    lax.fori_loop(1, np_, greet_column, 0)

    def dot(a, b, dims=None):
        if dims is None:
            return jnp.dot(a, b, preferred_element_type=F32)
        return lax.dot_general(a, b, dims, preferred_element_type=F32)

    t_in = fac[0:T_IN, :]
    t_out = fac[T_IN:T_ALL, :]
    gi = dot(t_in, t_in, TN)
    go = dot(t_out, t_out, TN)
    gram_out = go[0:64, 0:64] + go[64:128, 64:128]
    gl[0:64, :] = gi[0:64, :]
    gl[64:128, :] = jnp.concatenate([gram_out, gi[64:128, 64:128]], axis=1)
    tf[p] = fac[0:T_ALL, :]
    pl.semaphore_wait(barrier, ne + np_ - 2)

    piece = gl.shape[0] // ne

    def plane(phase, src, dst, o):
        return remote(
            src, dst.at[e], g_send.at[phase, o], g_recv.at[phase, e], spot(p, lax.rem(e + o, ne))
        )

    def plane_from(phase, src, dst, o):
        other = lax.rem(e + ne - o, ne)
        return remote(src, dst.at[other], g_send.at[phase, o], g_recv.at[phase, other], spot(p, other))

    def column(o):
        return remote(s1, g2.at[p], g_send.at[1, o], g_recv.at[1, p], spot(lax.rem(p + o, np_), e))

    def column_from(o):
        other = lax.rem(p + np_ - o, np_)
        return remote(s1, g2.at[other], g_send.at[1, o], g_recv.at[1, other], spot(other, e))

    def part_for(o):
        start = pl.multiple_of(lax.rem(e + o, ne) * piece, piece)
        return gl.at[pl.ds(start, piece)]

    def loop(low, high, body):
        def step(i, carry):
            body(i)
            return carry

        lax.fori_loop(low, high, step, 0)

    loop(1, ne, lambda o: plane(0, part_for(o), g1, o).start())
    g1[e] = gl[pl.ds(pl.multiple_of(e * piece, piece), piece), :]

    rows_of = (pl.ds(0, T_ALL // 2), pl.ds(T_ALL // 2, T_ALL // 2))

    def owner(k):
        s = (k + 1) // 2
        return lax.rem(z + jnp.where(k % 2 == 1, nz - s, s), nz)

    def pass_on(way, step):
        s = step if way == 1 else nz - step
        block = lax.rem(z + s, nz) * 2 + c
        ref = tf.at[block] if step < far - 1 else tf.at[block, rows_of[way]]
        return remote(ref, ref, t_send.at[way, step], t_recv.at[way, step], ring[way])

    def arrival(way, step):
        s = step + 1 if way == 1 else nz - step - 1
        block = lax.rem(z + s, nz) * 2 + c
        ref = tf.at[block] if step < far - 1 else tf.at[block, rows_of[way]]
        return remote(ref, ref, t_send.at[way, step], t_recv.at[way, step], ring[way])

    def across(k, core):
        ref = tf.at[owner(k) * 2 + core]
        return remote(ref, ref, sib_send.at[k], sib_recv.at[k], sibling)

    for way in (0, 1):
        pass_on(way, 0).start()
    across(0, c).start()

    width = mask.shape[0]
    cluster_q = lax.broadcasted_iota(jnp.int32, (width, query_ids.shape[1]), 0)
    hot_q = jnp.where(cluster_q == query_ids[...], 1.0, 0.0)
    cluster_t = lax.broadcasted_iota(jnp.int32, (width, train_ids.shape[1]), 0)
    hot_t = jnp.where(cluster_t == train_ids[...], 1.0, 0.0)
    picked = dot(mask[...].astype(F32).T.astype(BF16), hot_q.astype(BF16))
    allow[...] = dot(hot_t.T.astype(BF16), picked.astype(BF16))

    def total(ref, n):
        value = ref[0]
        for i in range(1, n):
            value = value + ref[i]
        return value

    loop(1, ne, lambda o: plane_from(0, gl.at[pl.ds(0, piece)], g1, o).wait_recv())
    s1[...] = total(g1, ne)
    loop(1, np_, lambda o: column(o).start())
    g2[p] = s1[...]

    def relay(step):
        for way in (0, 1):
            arrival(way, step - 1).wait_recv()
            if step < far:
                pass_on(way, step).start()
                across(2 * step - 1 + way, c).start()
        if step == far:
            across(nz - 1, c).start()

    relay(1)
    loop(1, np_, lambda o: column_from(o).wait_recv())
    s2[...] = total(g2, np_)
    loop(1, ne, lambda o: plane(2, s2, g3, o).start())
    g3[e] = s2[...]

    q_own = fac.at[pl.ds(T_ALL, Q_ALL)]

    def q_to(o):
        return remote(q_own, qf.at[e], q_send.at[o], q_recv.at[e], spot(p, lax.rem(e + o, ne)))

    def q_from(o):
        other = lax.rem(e + ne - o, ne)
        return remote(q_own, qf.at[other], q_send.at[o], q_recv.at[other], spot(p, other))

    loop(1, ne, lambda o: q_to(o).start())
    qf[e] = fac[T_ALL:ALL, :]

    for step in range(2, far + 1):
        relay(step)
    loop(1, ne, lambda o: plane_from(2, s2, g3, o).wait_recv())
    gram = jnp.concatenate([g3[i] for i in range(ne)], axis=0)
    upper = gram[0:64, 64:128]
    gram_in = jnp.concatenate(
        [gram[0:64, :], jnp.concatenate([upper.T, gram[64:128, 64:128]], axis=1)], axis=0
    )
    inv_in = inverse_of(gram_in, count)
    inv_out = inverse_of(gram[64:128, 0:64], count)
    zero = jnp.zeros((64, 64), F32)
    both = jnp.concatenate(
        [jnp.concatenate([inv_out, zero], axis=1), jnp.concatenate([zero, inv_out], axis=1)], axis=0
    )

    def split(x):
        high = x.astype(BF16)
        return high, (x - high.astype(F32)).astype(BF16)

    lane = lax.broadcasted_iota(jnp.int32, (8, 128), 1) // 16
    own_tokens = jnp.where(lane == lax.broadcasted_iota(jnp.int32, (8, 128), 0), 1.0, 0.0)

    def spreads(row, col):
        rows = [ot[col, pl.ds(row + r, 8, stride=0), :] * own_tokens for r in range(64)]
        return jnp.concatenate(rows, axis=0).astype(BF16)

    def put(dst, t0, a, b):
        for r in range(64):
            tile = jnp.concatenate([a[8 * r : 8 * r + 8], b[8 * r : 8 * r + 8]], axis=0)
            dst[pl.ds(t0, 16), 128 * r : 128 * (r + 1)] = tile.astype(BF16)

    def form(dst, t0, first, second):
        put(dst, t0, *(dot(spreads(row, col), inputs) for row, col, inputs in (first, second)))

    def form_train(g):
        for half in (0, 1):
            ot[half] = tf[g, T_IN + 128 * half : T_IN + 128 * (half + 1), :].astype(F32).T
        for h in (0, 1):
            form(
                tmat,
                pl.multiple_of(g * 32 + 16 * h, 16),
                (64 * h, 0, tf[g, 256 * h : 256 * h + 128, :]),
                (64 * h, 1, tf[g, 256 * h + 128 : 256 * h + 256, :]),
            )

    def train_two(k):
        form_train(owner(k) * 2 + c)
        across(k, 1 - c).wait_recv()
        form_train(owner(k) * 2 + 1 - c)

    loop(0, nz, train_two)

    def thirds(x):
        high = x.astype(BF16)
        mid, low = split(x - high.astype(F32))
        return high, mid, low

    in_parts, out_parts = thirds(inv_in), thirds(both)

    def apply(a, parts):
        return dot(a, parts[0]) + (dot(a, parts[1]) + dot(a, parts[2]))

    def form_query(i):
        side = apply(qf[i, Q_IN:Q_ALL, :], out_parts).T
        side_high = side.astype(BF16).astype(F32)
        ot[0] = side_high
        ot[1] = side - side_high
        high, low = split(apply(qf[i, 0:Q_IN, :], in_parts))
        wide = jnp.concatenate([high, low], axis=1)

        def product(h):
            rows = slice(128 * h, 128 * h + 128)
            main = dot(spreads(64 * h, 0), wide[rows])
            return main[:, 0:128] + (main[:, 128:256] + dot(spreads(64 * h, 1), high[rows]))

        put(qmat, pl.multiple_of(i * 16, 16), product(0), product(1))

    form_query(e)

    def query_other(o):
        q_from(o).wait_recv()
        form_query(lax.rem(e + ne - o, ne))

    loop(1, ne, query_other)

    deep = 1024
    raw[...] = jnp.zeros_like(raw)

    def contract(i):
        at = pl.ds(pl.multiple_of(i * deep, deep), deep)
        raw[...] += dot(tmat[:, at], qmat[:, at], NT)

    loop(0, tmat.shape[1] // deep, contract)
    block = raw[...] * scale * allow[...]
    scores[...] = block
    high, low = split(block)
    hot = hot_t.astype(BF16)
    partial = (dot(hot, high) + dot(hot, low)) * spread
    share = partial.T.astype(BF16)
    rows = share.shape[0] // ne
    for i in range(ne):
        cs[i] = share[i * rows : (i + 1) * rows, :]

    def c_to(o):
        other = lax.rem(e + o, ne)
        return remote(cs.at[other], cr.at[e], c_send.at[o], c_recv.at[e], spot(p, other))

    def c_from(o):
        other = lax.rem(e + ne - o, ne)
        return remote(cs.at[other], cr.at[other], c_send.at[o], c_recv.at[other], spot(p, other))

    loop(1, ne, lambda o: c_to(o).start())
    cr[e] = cs[e]
    loop(1, ne, lambda o: c_from(o).wait_recv())
    acc = cr[0].astype(F32)
    for i in range(1, ne):
        acc = acc + cr[i].astype(F32)
    sums[...] = acc

    def drain(o):
        plane(0, part_for(o), g1, o).wait_send()
        plane(2, s2, g3, o).wait_send()
        q_to(o).wait_send()
        c_to(o).wait_send()

    loop(1, ne, drain)
    loop(1, np_, lambda o: column(o).wait_send())
    for step in range(far):
        for way in (0, 1):
            pass_on(way, step).wait_send()
    loop(0, nz, lambda k: across(k, c).wait_send())


def solution(mesh):
    np_, ne = mesh.shape["param"], mesh.shape["ex"]
    nz = np_ // 2
    far = nz // 2

    def step(qa, qg, ta, tg, win, wout, query_clusters, train_clusters, pair_mask):
        groups, q_rows, tokens, feats = qa.shape
        t_rows = ta.shape[1]
        flat = [x.reshape(x.shape[0], x.shape[1] * x.shape[2], x.shape[3]) for x in (qa, qg, ta, tg)]
        any_space = pl.BlockSpec(memory_space=pl.ANY)
        vmem = pl.BlockSpec(memory_space=pltpu.VMEM)
        dma = pltpu.SemaphoreType.DMA
        limit = 63_000_000
        fac = pl.pallas_call(
            functools.partial(reduce_kernel, nz),
            out_shape=jax.ShapeDtypeStruct((ALL, 128), BF16),
            in_specs=[any_space] * 4 + [vmem] * 2,
            out_specs=vmem,
            scratch_shapes=[
                pltpu.VMEM((groups,) + flat[0].shape[1:], BF16),
                pltpu.VMEM((groups,) + flat[1].shape[1:], BF16),
                pltpu.VMEM((groups,) + flat[2].shape[1:], BF16),
                pltpu.VMEM((groups,) + flat[3].shape[1:], BF16),
                pltpu.VMEM((2, nz, T_ALL, 128), BF16),
                pltpu.VMEM((2, nz, Q_ALL, 128), F32),
                pltpu.VMEM((nz, T_ALL, 128), BF16),
                pltpu.VMEM((nz, Q_ALL, 128), F32),
                pltpu.VMEM((2, far, T_ALL, 128), BF16),
                pltpu.VMEM((2, far, Q_ALL, 128), F32),
                pltpu.VMEM((2, far, T_ALL, 128), BF16),
                pltpu.VMEM((2, far, Q_ALL, 128), F32),
                dma((4, groups)),
                dma((2, nz)),
                dma((2, nz)),
                dma((2, far, 2, 2)),
                dma((2, far, 2, 2)),
            ],
            compiler_params=pltpu.CompilerParams(
                collective_id=0, has_side_effects=True, vmem_limit_bytes=limit
            ),
            name="reduce_factors",
        )(*flat, win, wout.T)
        all_t, all_q = groups * t_rows, q_rows * ne
        dims = win.shape[1] * wout.shape[1]
        clusters = pair_mask.shape[0]
        total = groups * t_rows * ne
        scores, sums = pl.pallas_call(
            functools.partial(
                score_kernel,
                nz,
                ne,
                float(total * tokens),
                1.0 / (tokens * math.sqrt(dims)),
                math.sqrt(clusters / total),
            ),
            out_shape=(
                jax.ShapeDtypeStruct((all_t, all_q), F32),
                jax.ShapeDtypeStruct((q_rows, clusters), F32),
            ),
            in_specs=[vmem] * 4,
            out_specs=(vmem, vmem),
            scratch_shapes=[
                pltpu.VMEM((groups, T_ALL, 128), BF16),
                pltpu.VMEM((ne, Q_ALL, 128), BF16),
                pltpu.VMEM((128, 128), F32),
                pltpu.VMEM((ne, 128 // ne, 128), F32),
                pltpu.VMEM((np_, 128 // ne, 128), F32),
                pltpu.VMEM((ne, 128 // ne, 128), F32),
                pltpu.VMEM((128 // ne, 128), F32),
                pltpu.VMEM((128 // ne, 128), F32),
                pltpu.VMEM((all_t, dims), BF16),
                pltpu.VMEM((all_q, dims), BF16),
                pltpu.VMEM((2, 128, 128), F32),
                pltpu.VMEM((all_t, all_q), F32),
                pltpu.VMEM((all_t, all_q), F32),
                pltpu.VMEM((ne, q_rows, clusters), BF16),
                pltpu.VMEM((ne, q_rows, clusters), BF16),
                dma((3, max(ne, np_))),
                dma((3, max(ne, np_))),
                dma((ne,)),
                dma((ne,)),
                dma((2, far)),
                dma((2, far)),
                dma((nz,)),
                dma((nz,)),
                dma((ne,)),
                dma((ne,)),
            ],
            compiler_params=pltpu.CompilerParams(
                collective_id=1, has_side_effects=True, vmem_limit_bytes=limit
            ),
            name="score",
        )(fac, query_clusters, train_clusters.reshape(1, -1), pair_mask)
        return (
            scores.T.reshape(1, all_q, groups, t_rows),
            sums.reshape(1, q_rows, clusters),
        )

    return jax.shard_map(
        step,
        mesh=mesh,
        in_specs=(
            P(None, "ex", None, "param"),
            P(None, "ex", None, "param"),
            P(None, "ex", None, "param"),
            P(None, "ex", None, "param"),
            P("param", None),
            P("param", None),
            P("param", None),
            P(None, "ex"),
            P(),
        ),
        out_specs=(P("param", None, None, "ex"), P("param", "ex", None)),
        check_vma=False,
    )
```

```python
import functools
import math

import jax
import jax.numpy as jnp
from jax import lax
from jax.experimental import pallas as pl
from jax.experimental.pallas import tpu as pltpu
from jax.sharding import PartitionSpec as P

MESH = pl.DeviceIdType.MESH
F32 = jnp.float32
BF16 = jnp.bfloat16
NT = (((1,), (1,)), ((), ()))
TN = (((0,), (0,)), ((), ()))

T_IN, T_ALL = 512, 768
Q_IN, ALL = 256, 1152
Q_ALL = ALL - T_ALL


def remote(src, dst, send, recv, device):
    return pltpu.make_async_remote_copy(
        src_ref=src, dst_ref=dst, send_sem=send, recv_sem=recv, device_id=device, device_id_type=MESH
    )


def spot(p, e):
    return {"param": p, "ex": e}


def halves(chunk):
    size = (T_ALL, Q_ALL)[chunk] // 2
    return (pl.ds(0, size), pl.ds(size, size))


def reduce_kernel(
    nz,
    qa, qg, ta, tg, win, wout,
    out,
    qa_b, qg_b, ta_b, tg_b, part_t, part_q, sib_t, sib_q, snd_t, snd_q, rcv_t, rcv_q,
    in_sem, sib_send, sib_recv, ring_send, ring_recv,
):
    p, e = lax.axis_index("param"), lax.axis_index("ex")
    z, c = p // 2, p % 2
    sibling = spot(z * 2 + 1 - c, e)
    ring = (spot(lax.rem(z + 1, nz) * 2 + c, e), spot(lax.rem(z + nz - 1, nz) * 2 + c, e))
    far = nz // 2

    def shift(k):
        m = far - (k + 1) // 2
        return jnp.where(k % 2 == 1, m, nz - m) % nz

    def group(u):
        k = u // 2
        core = jnp.where(u % 2 == 0, 1 - c, c)
        return lax.rem(z + shift(k), nz) * 2 + core

    pairs = ((ta, ta_b), (tg, tg_b), (qa, qa_b), (qg, qg_b))

    def loads(u):
        g = group(u)
        return [
            pltpu.make_async_copy(src.at[g], dst.at[u], in_sem.at[i, u])
            for i, (src, dst) in enumerate(pairs)
        ]

    def start(u, carry):
        for copy in loads(u):
            copy.start()
        return carry

    lax.fori_loop(0, 2 * nz, start, 0)
    barrier = pltpu.get_barrier_semaphore()
    for device in (sibling,) + ring:
        pl.semaphore_signal(barrier, inc=1, device_id=device, device_id_type=MESH)
    pl.semaphore_wait(barrier, 3)

    w_in = win[...]
    narrow = wout[...].astype(F32).T
    blank = jnp.zeros_like(narrow)
    w_low = jnp.concatenate([narrow, blank], axis=1).astype(BF16)
    w_high = jnp.concatenate([blank, narrow], axis=1).astype(BF16)

    def dot(a, b):
        return jnp.dot(a, b, preferred_element_type=F32)

    parts, sibs, sends, recvs = (part_t, part_q), (sib_t, sib_q), (snd_t, snd_q), (rcv_t, rcv_q)

    def to_sibling(k, chunk):
        return remote(
            parts[chunk].at[0, k], sibs[chunk].at[k], sib_send.at[chunk, k], sib_recv.at[chunk, k], sibling
        )

    def project(u, carry):
        for copy in loads(u):
            copy.wait()
        k, own = u // 2, u % 2
        part_t[own, k, 0:T_IN, :] = dot(ta_b[u], w_in).astype(BF16)
        part_t[own, k, T_IN:T_ALL, :] = (
            dot(tg_b[u, 0:256, :], w_low) + dot(tg_b[u, 256:512, :], w_high)
        ).astype(BF16)

        @pl.when(own == 0)
        def _():
            to_sibling(k, 0).start()

        part_q[own, k, 0:Q_IN, :] = dot(qa_b[u], w_in)
        part_q[own, k, Q_IN:Q_ALL, :] = dot(qg_b[u, 0:128, :], w_low) + dot(qg_b[u, 128:256, :], w_high)

        @pl.when(own == 0)
        def _():
            to_sibling(k, 1).start()

        return carry

    def hop(way, step, chunk, half):
        rows = halves(chunk)[half]
        return remote(
            sends[chunk].at[way, step, rows],
            recvs[chunk].at[way, step, rows],
            ring_send.at[way, step, chunk, half],
            ring_recv.at[way, step, chunk, half],
            ring[way],
        )

    def own_sum(k, chunk, rows):
        return parts[chunk][1, k, rows, :].astype(F32) + sibs[chunk][k, rows, :].astype(F32)

    hops = []

    def send(way, step, chunk, half):
        rows = halves(chunk)[half]
        k = 0 if step == 0 else 2 * step - 1 + way
        value = own_sum(k, chunk, rows)
        if step >= 2 or (step == 1 and half == way):
            hop(way, step - 1, chunk, half).wait_recv()
            value = value + recvs[chunk][way, step - 1, rows, :].astype(F32)
        sends[chunk][way, step, rows, :] = value.astype(sends[chunk].dtype)
        copy = hop(way, step, chunk, half)
        copy.start()
        hops.append(copy)

    def round_of(step, chunk):
        if step == 0:
            for way in (0, 1):
                send(way, 0, chunk, way)
            return
        for late in (1, 0):
            for way in (0, 1):
                send(way, step, chunk, way if late == 0 else 1 - way)

    for step in range(far):
        low, high = (0, 2) if step == 0 else (4 * step - 2, 4 * step + 2)
        lax.fori_loop(low, high, project, 0)
        for k in range(low // 2, high // 2):
            to_sibling(k, 0).wait_recv()
            to_sibling(k, 1).wait_recv()
        round_of(step, 0)
    round_of(0, 1)
    lax.fori_loop(2 * nz - 2, 2 * nz, project, 0)
    to_sibling(nz - 1, 0).wait_recv()
    to_sibling(nz - 1, 1).wait_recv()

    def final(chunk):
        for half in (1, 0):
            rows = halves(chunk)[half]
            value = own_sum(nz - 1, chunk, rows)
            for way in (0, 1):
                hop(way, far - 1, chunk, half).wait_recv()
                value = value + recvs[chunk][way, far - 1, rows, :].astype(F32)
            out[pl.ds(T_ALL * chunk + rows.start, rows.size), :] = value.astype(BF16)

    for step in range(1, far):
        round_of(step, 1)
    final(0)
    final(1)
    for copy in hops:
        copy.wait_send()
    for k in range(nz):
        to_sibling(k, 0).wait_send()
        to_sibling(k, 1).wait_send()


def newton(damped, level, steps, scalings):
    size = damped.shape[0]
    rows = lax.broadcasted_iota(jnp.int32, (size, size), 0)
    eye = (rows == lax.broadcasted_iota(jnp.int32, (size, size), 1)).astype(F32)

    def dot(a, b):
        return jnp.dot(a, b, preferred_element_type=F32, precision=lax.Precision.HIGHEST)

    resid = eye - level * damped
    guess = level * eye
    for index in range(steps):
        c = scalings[index]
        grown = guess + (level * resid if index == 0 else dot(guess, resid))
        resid = (1.0 - c) * eye + c * dot(resid, resid)
        guess = c * grown
    for _ in range(2):
        resid = eye - dot(damped, guess)
        guess = guess + dot(guess, resid)
    return 0.5 * (guess + guess.T)


def schedule_of(size):
    kappa = 1.0 + 10.0 * size
    rho = (kappa - 1.0) / (kappa + 1.0)
    scalings = []
    while rho > 1e-4:
        scalings.append(2.0 / (2.0 - rho * rho))
        rho = rho * rho / (2.0 - rho * rho)
    return 2.0 / (1.0 + kappa), scalings


def inverse_of(gram, count):
    size = gram.shape[0]
    mean = gram * (1.0 / count)
    rows = lax.broadcasted_iota(jnp.int32, (size, size), 0)
    diagonal = rows == lax.broadcasted_iota(jnp.int32, (size, size), 1)
    floor = 0.1 / size * jnp.sum(jnp.where(diagonal, mean, 0.0), keepdims=True)
    damped = mean + jnp.where(diagonal, floor, 0.0)
    level, scalings = schedule_of(size)
    return newton(damped, level / floor, len(scalings), scalings)


def score_kernel(
    nz, ne, count, scale, spread,
    fac, query_ids, train_ids, mask,
    scores, sums,
    tf, qf, gl, g1, g2, g3, s1, s2, tmat, qmat, ot, raw, allow, cs, cr,
    g_send, g_recv, q_send, q_recv, t_send, t_recv, sib_send, sib_recv, c_send, c_recv,
):
    p, e = lax.axis_index("param"), lax.axis_index("ex")
    np_ = 2 * nz
    z, c = p // 2, p % 2
    sibling = spot(z * 2 + 1 - c, e)
    ring = (spot(lax.rem(z + 1, nz) * 2 + c, e), spot(lax.rem(z + nz - 1, nz) * 2 + c, e))
    far = nz // 2

    barrier = pltpu.get_barrier_semaphore()

    def greet(o, carry):
        pl.semaphore_signal(barrier, inc=1, device_id=spot(p, lax.rem(e + o, ne)), device_id_type=MESH)
        return carry

    def greet_column(o, carry):
        pl.semaphore_signal(barrier, inc=1, device_id=spot(lax.rem(p + o, np_), e), device_id_type=MESH)
        return carry

    lax.fori_loop(1, ne, greet, 0)
    lax.fori_loop(1, np_, greet_column, 0)

    def dot(a, b, dims=None):
        if dims is None:
            return jnp.dot(a, b, preferred_element_type=F32)
        return lax.dot_general(a, b, dims, preferred_element_type=F32)

    t_in = fac[0:T_IN, :]
    t_out = fac[T_IN:T_ALL, :]
    gi = dot(t_in, t_in, TN)
    go = dot(t_out, t_out, TN)
    gram_out = go[0:64, 0:64] + go[64:128, 64:128]
    gl[0:64, :] = gi[0:64, :]
    gl[64:128, :] = jnp.concatenate([gram_out, gi[64:128, 64:128]], axis=1)
    tf[p] = fac[0:T_ALL, :]
    pl.semaphore_wait(barrier, ne + np_ - 2)

    piece = gl.shape[0] // ne

    def plane(phase, src, dst, o):
        return remote(
            src, dst.at[e], g_send.at[phase, o], g_recv.at[phase, e], spot(p, lax.rem(e + o, ne))
        )

    def plane_from(phase, src, dst, o):
        other = lax.rem(e + ne - o, ne)
        return remote(src, dst.at[other], g_send.at[phase, o], g_recv.at[phase, other], spot(p, other))

    def column(o):
        return remote(s1, g2.at[p], g_send.at[1, o], g_recv.at[1, p], spot(lax.rem(p + o, np_), e))

    def column_from(o):
        other = lax.rem(p + np_ - o, np_)
        return remote(s1, g2.at[other], g_send.at[1, o], g_recv.at[1, other], spot(other, e))

    def part_for(o):
        start = pl.multiple_of(lax.rem(e + o, ne) * piece, piece)
        return gl.at[pl.ds(start, piece)]

    def loop(low, high, body):
        def step(i, carry):
            body(i)
            return carry

        lax.fori_loop(low, high, step, 0)

    loop(1, ne, lambda o: plane(0, part_for(o), g1, o).start())
    g1[e] = gl[pl.ds(pl.multiple_of(e * piece, piece), piece), :]

    rows_of = (pl.ds(0, T_ALL // 2), pl.ds(T_ALL // 2, T_ALL // 2))

    def owner(k):
        s = (k + 1) // 2
        return lax.rem(z + jnp.where(k % 2 == 1, nz - s, s), nz)

    def pass_on(way, step):
        s = step if way == 1 else nz - step
        block = lax.rem(z + s, nz) * 2 + c
        ref = tf.at[block] if step < far - 1 else tf.at[block, rows_of[way]]
        return remote(ref, ref, t_send.at[way, step], t_recv.at[way, step], ring[way])

    def arrival(way, step):
        s = step + 1 if way == 1 else nz - step - 1
        block = lax.rem(z + s, nz) * 2 + c
        ref = tf.at[block] if step < far - 1 else tf.at[block, rows_of[way]]
        return remote(ref, ref, t_send.at[way, step], t_recv.at[way, step], ring[way])

    def across(k, core):
        ref = tf.at[owner(k) * 2 + core]
        return remote(ref, ref, sib_send.at[k], sib_recv.at[k], sibling)

    for way in (0, 1):
        pass_on(way, 0).start()
    across(0, c).start()

    edge = math.isqrt(ne)
    half = Q_ALL // 2

    def place(o, da, db):
        a, b = (e // edge, e % edge) if o == 0 else (e % edge, e // edge)
        a, b = lax.rem(a + da + edge, edge), lax.rem(b + db + edge, edge)
        return a * edge + b if o == 0 else b * edge + a

    along = (0, -1, 1, 2)

    def q_copy(o, way, slot, sending):
        back = 0 if sending else (-1 if way == 0 else 1)
        sign = 1 if way == 0 else -1
        rows = pl.ds(half * o, half)
        if slot == 0:
            block, target = place(o, back, 0), place(o, sign, 0)
        elif slot == 1:
            block, target = place(o, back - sign, 0), place(o, sign, 0)
            rows = pl.ds(half * o + half // 2 * way, half // 2)
        elif slot < 6:
            block, target = place(o, along[slot - 2], back), place(o, 0, sign)
        else:
            block, target = place(o, along[2 * way + slot - 6], back - sign), place(o, 0, sign)
        ref = qf.at[block, rows]
        return remote(ref, ref, q_send.at[o, way, slot], q_recv.at[o, way, slot], spot(p, target))

    both_ways = [(o, way) for o in (0, 1) for way in (0, 1)]

    def q_start(*slots):
        for slot in slots:
            for o, way in both_ways:
                q_copy(o, way, slot, True).start()

    def q_wait(*slots):
        for slot in slots:
            for o, way in both_ways:
                q_copy(o, way, slot, False).wait_recv()

    qf[e] = fac[T_ALL:ALL, :]

    q_start(0, 2)

    width = mask.shape[0]
    cluster_q = lax.broadcasted_iota(jnp.int32, (width, query_ids.shape[1]), 0)
    hot_q = jnp.where(cluster_q == query_ids[...], 1.0, 0.0)
    cluster_t = lax.broadcasted_iota(jnp.int32, (width, train_ids.shape[1]), 0)
    hot_t = jnp.where(cluster_t == train_ids[...], 1.0, 0.0)
    picked = dot(mask[...].astype(F32).T.astype(BF16), hot_q.astype(BF16))
    allow[...] = dot(hot_t.T.astype(BF16), picked.astype(BF16))

    def total(ref, n):
        value = ref[0]
        for i in range(1, n):
            value = value + ref[i]
        return value

    loop(1, ne, lambda o: plane_from(0, gl.at[pl.ds(0, piece)], g1, o).wait_recv())
    s1[...] = total(g1, ne)
    loop(1, np_, lambda o: column(o).start())
    g2[p] = s1[...]

    def relay(step):
        for way in (0, 1):
            arrival(way, step - 1).wait_recv()
            if step < far:
                pass_on(way, step).start()
                across(2 * step - 1 + way, c).start()
        if step == far:
            across(nz - 1, c).start()

    q_wait(0)
    q_start(1, 3, 4)
    relay(1)
    q_wait(1)
    q_start(5)
    loop(1, np_, lambda o: column_from(o).wait_recv())
    s2[...] = total(g2, np_)
    loop(1, ne, lambda o: plane(2, s2, g3, o).start())
    g3[e] = s2[...]

    relay(2)
    for o in (0, 1):
        for way in (0, 1):
            for index in (0, 1):
                q_copy(o, way, 2 + 2 * way + index, False).wait_recv()
                q_copy(o, way, 6 + index, True).start()
    for step in range(3, far + 1):
        relay(step)
    loop(1, ne, lambda o: plane_from(2, s2, g3, o).wait_recv())
    gram = jnp.concatenate([g3[i] for i in range(ne)], axis=0)
    upper = gram[0:64, 64:128]
    gram_in = jnp.concatenate(
        [gram[0:64, :], jnp.concatenate([upper.T, gram[64:128, 64:128]], axis=1)], axis=0
    )
    inv_in = inverse_of(gram_in, count)
    inv_out = inverse_of(gram[64:128, 0:64], count)
    zero = jnp.zeros((64, 64), F32)
    both = jnp.concatenate(
        [jnp.concatenate([inv_out, zero], axis=1), jnp.concatenate([zero, inv_out], axis=1)], axis=0
    )

    def split(x):
        high = x.astype(BF16)
        return high, (x - high.astype(F32)).astype(BF16)

    lane = lax.broadcasted_iota(jnp.int32, (8, 128), 1) // 16
    own_tokens = jnp.where(lane == lax.broadcasted_iota(jnp.int32, (8, 128), 0), 1.0, 0.0)

    def spreads(row, col):
        rows = [ot[col, pl.ds(row + r, 8, stride=0), :] * own_tokens for r in range(64)]
        return jnp.concatenate(rows, axis=0).astype(BF16)

    def put(dst, t0, a, b):
        for r in range(64):
            tile = jnp.concatenate([a[8 * r : 8 * r + 8], b[8 * r : 8 * r + 8]], axis=0)
            dst[pl.ds(t0, 16), 128 * r : 128 * (r + 1)] = tile.astype(BF16)

    def form(dst, t0, first, second):
        put(dst, t0, *(dot(spreads(row, col), inputs) for row, col, inputs in (first, second)))

    def form_train(g):
        for half in (0, 1):
            ot[half] = tf[g, T_IN + 128 * half : T_IN + 128 * (half + 1), :].astype(F32).T
        for h in (0, 1):
            form(
                tmat,
                pl.multiple_of(g * 32 + 16 * h, 16),
                (64 * h, 0, tf[g, 256 * h : 256 * h + 128, :]),
                (64 * h, 1, tf[g, 256 * h + 128 : 256 * h + 256, :]),
            )

    def train_two(k):
        form_train(owner(k) * 2 + c)
        across(k, 1 - c).wait_recv()
        form_train(owner(k) * 2 + 1 - c)

    loop(0, nz, train_two)

    def thirds(x):
        high = x.astype(BF16)
        mid, low = split(x - high.astype(F32))
        return high, mid, low

    in_parts, out_parts = thirds(inv_in), thirds(both)

    def apply(a, parts):
        return dot(a, parts[0]) + (dot(a, parts[1]) + dot(a, parts[2]))

    def form_query(i):
        side = apply(qf[i, Q_IN:Q_ALL, :], out_parts).T
        side_high = side.astype(BF16).astype(F32)
        ot[0] = side_high
        ot[1] = side - side_high
        high, low = split(apply(qf[i, 0:Q_IN, :], in_parts))
        wide = jnp.concatenate([high, low], axis=1)

        def product(h):
            rows = slice(128 * h, 128 * h + 128)
            main = dot(spreads(64 * h, 0), wide[rows])
            return main[:, 0:128] + (main[:, 128:256] + dot(spreads(64 * h, 1), high[rows]))

        put(qmat, pl.multiple_of(i * 16, 16), product(0), product(1))

    for o in (0, 1):
        for way in (0, 1):
            for slot in (4 - 2 * way, 5 - 2 * way, 6, 7):
                q_copy(o, way, slot, False).wait_recv()
    loop(0, ne, form_query)

    deep = 1024
    raw[...] = jnp.zeros_like(raw)

    def contract(i):
        at = pl.ds(pl.multiple_of(i * deep, deep), deep)
        raw[...] += dot(tmat[:, at], qmat[:, at], NT)

    loop(0, tmat.shape[1] // deep, contract)
    block = raw[...] * scale * allow[...]
    scores[...] = block
    high, low = split(block)
    hot = hot_t.astype(BF16)
    partial = (dot(hot, high) + dot(hot, low)) * spread
    share = partial.T.astype(BF16)
    rows = share.shape[0] // ne
    for i in range(ne):
        cs[i] = share[i * rows : (i + 1) * rows, :]

    def c_to(o):
        other = lax.rem(e + o, ne)
        return remote(cs.at[other], cr.at[e], c_send.at[o], c_recv.at[e], spot(p, other))

    def c_from(o):
        other = lax.rem(e + ne - o, ne)
        return remote(cs.at[other], cr.at[other], c_send.at[o], c_recv.at[other], spot(p, other))

    loop(1, ne, lambda o: c_to(o).start())
    cr[e] = cs[e]
    loop(1, ne, lambda o: c_from(o).wait_recv())
    acc = cr[0].astype(F32)
    for i in range(1, ne):
        acc = acc + cr[i].astype(F32)
    sums[...] = acc

    def drain(o):
        plane(0, part_for(o), g1, o).wait_send()
        plane(2, s2, g3, o).wait_send()
        c_to(o).wait_send()

    loop(1, ne, drain)
    for o, way in both_ways:
        for slot in range(8):
            q_copy(o, way, slot, True).wait_send()
    loop(1, np_, lambda o: column(o).wait_send())
    for step in range(far):
        for way in (0, 1):
            pass_on(way, step).wait_send()
    loop(0, nz, lambda k: across(k, c).wait_send())


def solution(mesh):
    np_, ne = mesh.shape["param"], mesh.shape["ex"]
    nz = np_ // 2
    far = nz // 2

    def step(qa, qg, ta, tg, win, wout, query_clusters, train_clusters, pair_mask):
        groups, q_rows, tokens, feats = qa.shape
        t_rows = ta.shape[1]
        flat = [x.reshape(x.shape[0], x.shape[1] * x.shape[2], x.shape[3]) for x in (qa, qg, ta, tg)]
        any_space = pl.BlockSpec(memory_space=pl.ANY)
        vmem = pl.BlockSpec(memory_space=pltpu.VMEM)
        dma = pltpu.SemaphoreType.DMA
        limit = 63_000_000
        fac = pl.pallas_call(
            functools.partial(reduce_kernel, nz),
            out_shape=jax.ShapeDtypeStruct((ALL, 128), BF16),
            in_specs=[any_space] * 4 + [vmem] * 2,
            out_specs=vmem,
            scratch_shapes=[
                pltpu.VMEM((groups,) + flat[0].shape[1:], BF16),
                pltpu.VMEM((groups,) + flat[1].shape[1:], BF16),
                pltpu.VMEM((groups,) + flat[2].shape[1:], BF16),
                pltpu.VMEM((groups,) + flat[3].shape[1:], BF16),
                pltpu.VMEM((2, nz, T_ALL, 128), BF16),
                pltpu.VMEM((2, nz, Q_ALL, 128), F32),
                pltpu.VMEM((nz, T_ALL, 128), BF16),
                pltpu.VMEM((nz, Q_ALL, 128), F32),
                pltpu.VMEM((2, far, T_ALL, 128), BF16),
                pltpu.VMEM((2, far, Q_ALL, 128), F32),
                pltpu.VMEM((2, far, T_ALL, 128), BF16),
                pltpu.VMEM((2, far, Q_ALL, 128), F32),
                dma((4, groups)),
                dma((2, nz)),
                dma((2, nz)),
                dma((2, far, 2, 2)),
                dma((2, far, 2, 2)),
            ],
            compiler_params=pltpu.CompilerParams(
                collective_id=0, has_side_effects=True, vmem_limit_bytes=limit
            ),
            name="reduce_factors",
        )(*flat, win, wout.T)
        all_t, all_q = groups * t_rows, q_rows * ne
        dims = win.shape[1] * wout.shape[1]
        clusters = pair_mask.shape[0]
        total = groups * t_rows * ne
        scores, sums = pl.pallas_call(
            functools.partial(
                score_kernel,
                nz,
                ne,
                float(total * tokens),
                1.0 / (tokens * math.sqrt(dims)),
                math.sqrt(clusters / total),
            ),
            out_shape=(
                jax.ShapeDtypeStruct((all_t, all_q), F32),
                jax.ShapeDtypeStruct((q_rows, clusters), F32),
            ),
            in_specs=[vmem] * 4,
            out_specs=(vmem, vmem),
            scratch_shapes=[
                pltpu.VMEM((groups, T_ALL, 128), BF16),
                pltpu.VMEM((ne, Q_ALL, 128), BF16),
                pltpu.VMEM((128, 128), F32),
                pltpu.VMEM((ne, 128 // ne, 128), F32),
                pltpu.VMEM((np_, 128 // ne, 128), F32),
                pltpu.VMEM((ne, 128 // ne, 128), F32),
                pltpu.VMEM((128 // ne, 128), F32),
                pltpu.VMEM((128 // ne, 128), F32),
                pltpu.VMEM((all_t, dims), BF16),
                pltpu.VMEM((all_q, dims), BF16),
                pltpu.VMEM((2, 128, 128), F32),
                pltpu.VMEM((all_t, all_q), F32),
                pltpu.VMEM((all_t, all_q), F32),
                pltpu.VMEM((ne, q_rows, clusters), BF16),
                pltpu.VMEM((ne, q_rows, clusters), BF16),
                dma((3, max(ne, np_))),
                dma((3, max(ne, np_))),
                dma((2, 2, 8)),
                dma((2, 2, 8)),
                dma((2, far)),
                dma((2, far)),
                dma((nz,)),
                dma((nz,)),
                dma((ne,)),
                dma((ne,)),
            ],
            compiler_params=pltpu.CompilerParams(
                collective_id=1, has_side_effects=True, vmem_limit_bytes=limit
            ),
            name="score",
        )(fac, query_clusters, train_clusters.reshape(1, -1), pair_mask)
        return (
            scores.T.reshape(1, all_q, groups, t_rows),
            sums.reshape(1, q_rows, clusters),
        )

    return jax.shard_map(
        step,
        mesh=mesh,
        in_specs=(
            P(None, "ex", None, "param"),
            P(None, "ex", None, "param"),
            P(None, "ex", None, "param"),
            P(None, "ex", None, "param"),
            P("param", None),
            P("param", None),
            P("param", None),
            P(None, "ex"),
            P(),
        ),
        out_specs=(P("param", None, None, "ex"), P("param", "ex", None)),
        check_vma=False,
    )
```

```python
import functools
import math

import jax
import jax.numpy as jnp
from jax import lax
from jax.experimental import pallas as pl
from jax.experimental.pallas import tpu as pltpu
from jax.sharding import PartitionSpec as P

MESH = pl.DeviceIdType.MESH
F32 = jnp.float32
BF16 = jnp.bfloat16
NT = (((1,), (1,)), ((), ()))
TN = (((0,), (0,)), ((), ()))

T_IN, T_ALL = 512, 768
Q_IN, ALL = 256, 1152
Q_ALL = ALL - T_ALL


def remote(src, dst, send, recv, device):
    return pltpu.make_async_remote_copy(
        src_ref=src, dst_ref=dst, send_sem=send, recv_sem=recv, device_id=device, device_id_type=MESH
    )


def spot(p, e):
    return {"param": p, "ex": e}


def halves(chunk):
    size = (T_ALL, Q_ALL)[chunk] // 2
    return (pl.ds(0, size), pl.ds(size, size))


def newton(damped, level, steps, scalings):
    size = damped.shape[0]
    rows = lax.broadcasted_iota(jnp.int32, (size, size), 0)
    eye = (rows == lax.broadcasted_iota(jnp.int32, (size, size), 1)).astype(F32)

    def dot(a, b):
        return jnp.dot(a, b, preferred_element_type=F32, precision=lax.Precision.HIGHEST)

    resid = eye - level * damped
    guess = level * eye
    for index in range(steps):
        c = scalings[index]
        grown = guess + (level * resid if index == 0 else dot(guess, resid))
        resid = (1.0 - c) * eye + c * dot(resid, resid)
        guess = c * grown
    for _ in range(2):
        resid = eye - dot(damped, guess)
        guess = guess + dot(guess, resid)
    return 0.5 * (guess + guess.T)


def schedule_of(size):
    kappa = 1.0 + 10.0 * size
    rho = (kappa - 1.0) / (kappa + 1.0)
    scalings = []
    while rho > 1e-4:
        scalings.append(2.0 / (2.0 - rho * rho))
        rho = rho * rho / (2.0 - rho * rho)
    return 2.0 / (1.0 + kappa), scalings


def inverse_of(gram, count):
    size = gram.shape[0]
    mean = gram * (1.0 / count)
    rows = lax.broadcasted_iota(jnp.int32, (size, size), 0)
    diagonal = rows == lax.broadcasted_iota(jnp.int32, (size, size), 1)
    floor = 0.1 / size * jnp.sum(jnp.where(diagonal, mean, 0.0), keepdims=True)
    damped = mean + jnp.where(diagonal, floor, 0.0)
    level, scalings = schedule_of(size)
    return newton(damped, level / floor, len(scalings), scalings)


def kernel(
    nz, ne, count, scale, spread,
    qa, qg, ta, tg, win, wout, query_ids, train_ids, mask,
    scores, sums,
    qa_b, qg_b, ta_b, tg_b, part_t, part_q, sib_t, sib_q, snd_t, snd_q, rcv_t, rcv_q,
    tf, qf, gl, g1, g2, g3, s1, s2, tmat, qmat, ot, raw, allow, cs, cr,
    in_sem, sib_send, sib_recv, ring_send, ring_recv,
    g_send, g_recv, q_send, q_recv, t_send, t_recv, over_send, over_recv, c_send, c_recv,
):
    p, e = lax.axis_index("param"), lax.axis_index("ex")
    np_ = 2 * nz
    z, c = p // 2, p % 2
    sibling = spot(z * 2 + 1 - c, e)
    ring = (spot(lax.rem(z + 1, nz) * 2 + c, e), spot(lax.rem(z + nz - 1, nz) * 2 + c, e))
    far = nz // 2

    def shift(k):
        m = far - (k + 1) // 2
        return jnp.where(k % 2 == 1, m, nz - m) % nz

    def group(u):
        k = u // 2
        core = jnp.where(u % 2 == 0, 1 - c, c)
        return lax.rem(z + shift(k), nz) * 2 + core

    pairs = ((ta, ta_b), (tg, tg_b), (qa, qa_b), (qg, qg_b))

    def loads(u):
        g = group(u)
        return [
            pltpu.make_async_copy(src.at[g], dst.at[u], in_sem.at[i, u])
            for i, (src, dst) in enumerate(pairs)
        ]

    def start(u, carry):
        for copy in loads(u):
            copy.start()
        return carry

    lax.fori_loop(0, 2 * nz, start, 0)
    barrier = pltpu.get_barrier_semaphore()

    def greet(o, carry):
        pl.semaphore_signal(barrier, inc=1, device_id=spot(p, lax.rem(e + o, ne)), device_id_type=MESH)
        return carry

    def greet_column(o, carry):
        pl.semaphore_signal(barrier, inc=1, device_id=spot(lax.rem(p + o, np_), e), device_id_type=MESH)
        return carry

    lax.fori_loop(1, ne, greet, 0)
    lax.fori_loop(1, np_, greet_column, 0)

    def dot(a, b, dims=None):
        if dims is None:
            return jnp.dot(a, b, preferred_element_type=F32)
        return lax.dot_general(a, b, dims, preferred_element_type=F32)

    width = mask.shape[0]
    cluster_q = lax.broadcasted_iota(jnp.int32, (width, query_ids.shape[1]), 0)
    hot_q = jnp.where(cluster_q == query_ids[...], 1.0, 0.0)
    cluster_t = lax.broadcasted_iota(jnp.int32, (width, train_ids.shape[1]), 0)
    hot_t = jnp.where(cluster_t == train_ids[...], 1.0, 0.0)
    picked = dot(mask[...].astype(F32).T.astype(BF16), hot_q.astype(BF16))
    allow[...] = dot(hot_t.T.astype(BF16), picked.astype(BF16))

    pl.semaphore_wait(barrier, ne + np_ - 2)

    w_in = win[...]
    narrow = wout[...].astype(F32).T
    blank = jnp.zeros_like(narrow)
    w_low = jnp.concatenate([narrow, blank], axis=1).astype(BF16)
    w_high = jnp.concatenate([blank, narrow], axis=1).astype(BF16)

    parts, sibs, sends, recvs = (part_t, part_q), (sib_t, sib_q), (snd_t, snd_q), (rcv_t, rcv_q)

    def to_sibling(k, chunk):
        return remote(
            parts[chunk].at[0, k], sibs[chunk].at[k], sib_send.at[chunk, k], sib_recv.at[chunk, k], sibling
        )

    def project(u, carry):
        for copy in loads(u):
            copy.wait()
        k, own = u // 2, u % 2
        part_t[own, k, 0:T_IN, :] = dot(ta_b[u], w_in).astype(BF16)
        part_t[own, k, T_IN:T_ALL, :] = (
            dot(tg_b[u, 0:256, :], w_low) + dot(tg_b[u, 256:512, :], w_high)
        ).astype(BF16)

        @pl.when(own == 0)
        def _():
            to_sibling(k, 0).start()

        part_q[own, k, 0:Q_IN, :] = dot(qa_b[u], w_in)
        part_q[own, k, Q_IN:Q_ALL, :] = dot(qg_b[u, 0:128, :], w_low) + dot(qg_b[u, 128:256, :], w_high)

        @pl.when(own == 0)
        def _():
            to_sibling(k, 1).start()

        return carry

    def hop(way, step, chunk, half):
        rows = halves(chunk)[half]
        return remote(
            sends[chunk].at[way, step, rows],
            recvs[chunk].at[way, step, rows],
            ring_send.at[way, step, chunk, half],
            ring_recv.at[way, step, chunk, half],
            ring[way],
        )

    def own_sum(k, chunk, rows):
        return parts[chunk][1, k, rows, :].astype(F32) + sibs[chunk][k, rows, :].astype(F32)

    hops = []

    def send(way, step, chunk, half):
        rows = halves(chunk)[half]
        k = 0 if step == 0 else 2 * step - 1 + way
        value = own_sum(k, chunk, rows)
        if step >= 2 or (step == 1 and half == way):
            hop(way, step - 1, chunk, half).wait_recv()
            value = value + recvs[chunk][way, step - 1, rows, :].astype(F32)
        sends[chunk][way, step, rows, :] = value.astype(sends[chunk].dtype)
        copy = hop(way, step, chunk, half)
        copy.start()
        hops.append(copy)

    def short(step, chunk):
        for way in (0, 1):
            send(way, step, chunk, 1 - way)

    def long(step, chunk):
        for way in (0, 1):
            send(way, step, chunk, way)

    def final(chunk, put):
        for index in (1, 0):
            rows = halves(chunk)[index]
            value = own_sum(nz - 1, chunk, rows)
            for way in (0, 1):
                hop(way, far - 1, chunk, index).wait_recv()
                value = value + recvs[chunk][way, far - 1, rows, :].astype(F32)
            put(rows, value.astype(BF16))

    piece = gl.shape[0] // ne

    def plane(phase, src, dst, o):
        return remote(
            src, dst.at[e], g_send.at[phase, o], g_recv.at[phase, e], spot(p, lax.rem(e + o, ne))
        )

    def plane_from(phase, src, dst, o):
        other = lax.rem(e + ne - o, ne)
        return remote(src, dst.at[other], g_send.at[phase, o], g_recv.at[phase, other], spot(p, other))

    def column(o):
        return remote(s1, g2.at[p], g_send.at[1, o], g_recv.at[1, p], spot(lax.rem(p + o, np_), e))

    def column_from(o):
        other = lax.rem(p + np_ - o, np_)
        return remote(s1, g2.at[other], g_send.at[1, o], g_recv.at[1, other], spot(other, e))

    def part_for(o):
        start = pl.multiple_of(lax.rem(e + o, ne) * piece, piece)
        return gl.at[pl.ds(start, piece)]

    def loop(low, high, body):
        def step(i, carry):
            body(i)
            return carry

        lax.fori_loop(low, high, step, 0)

    rows_of = (pl.ds(0, T_ALL // 2), pl.ds(T_ALL // 2, T_ALL // 2))

    def owner(k):
        s = (k + 1) // 2
        return lax.rem(z + jnp.where(k % 2 == 1, nz - s, s), nz)

    def pass_on(way, step):
        s = step if way == 1 else nz - step
        block = lax.rem(z + s, nz) * 2 + c
        ref = tf.at[block] if step < far - 1 else tf.at[block, rows_of[way]]
        return remote(ref, ref, t_send.at[way, step], t_recv.at[way, step], ring[way])

    def arrival(way, step):
        s = step + 1 if way == 1 else nz - step - 1
        block = lax.rem(z + s, nz) * 2 + c
        ref = tf.at[block] if step < far - 1 else tf.at[block, rows_of[way]]
        return remote(ref, ref, t_send.at[way, step], t_recv.at[way, step], ring[way])

    def across(k, core):
        ref = tf.at[owner(k) * 2 + core]
        return remote(ref, ref, over_send.at[k], over_recv.at[k], sibling)

    edge = math.isqrt(ne)
    half = Q_ALL // 2

    def place(o, da, db):
        a, b = (e // edge, e % edge) if o == 0 else (e % edge, e // edge)
        a, b = lax.rem(a + da + edge, edge), lax.rem(b + db + edge, edge)
        return a * edge + b if o == 0 else b * edge + a

    along = (0, -1, 1, 2)

    def q_copy(o, way, slot, sending):
        back = 0 if sending else (-1 if way == 0 else 1)
        sign = 1 if way == 0 else -1
        rows = pl.ds(half * o, half)
        if slot == 0:
            block, target = place(o, back, 0), place(o, sign, 0)
        elif slot == 1:
            block, target = place(o, back - sign, 0), place(o, sign, 0)
            rows = pl.ds(half * o + half // 2 * way, half // 2)
        elif slot < 6:
            block, target = place(o, along[slot - 2], back), place(o, 0, sign)
        else:
            block, target = place(o, along[2 * way + slot - 6], back - sign), place(o, 0, sign)
        ref = qf.at[block, rows]
        return remote(ref, ref, q_send.at[o, way, slot], q_recv.at[o, way, slot], spot(p, target))

    both_ways = [(o, way) for o in (0, 1) for way in (0, 1)]

    def q_start(*slots):
        for slot in slots:
            for o, way in both_ways:
                q_copy(o, way, slot, True).start()

    def q_wait(*slots):
        for slot in slots:
            for o, way in both_ways:
                q_copy(o, way, slot, False).wait_recv()

    def total(ref, n):
        value = ref[0]
        for i in range(1, n):
            value = value + ref[i]
        return value

    def relay(step):
        for way in (0, 1):
            arrival(way, step - 1).wait_recv()
            if step < far:
                pass_on(way, step).start()
                across(2 * step - 1 + way, c).start()
        if step == far:
            across(nz - 1, c).start()

    def split(x):
        high = x.astype(BF16)
        return high, (x - high.astype(F32)).astype(BF16)

    lane = lax.broadcasted_iota(jnp.int32, (8, 128), 1) // 16
    own_tokens = jnp.where(lane == lax.broadcasted_iota(jnp.int32, (8, 128), 0), 1.0, 0.0)

    def spreads(row, col):
        rows = [ot[col, pl.ds(row + r, 8, stride=0), :] * own_tokens for r in range(64)]
        return jnp.concatenate(rows, axis=0).astype(BF16)

    def put(dst, t0, a, b):
        for r in range(64):
            tile = jnp.concatenate([a[8 * r : 8 * r + 8], b[8 * r : 8 * r + 8]], axis=0)
            dst[pl.ds(t0, 16), 128 * r : 128 * (r + 1)] = tile.astype(BF16)

    def form(dst, t0, first, second):
        put(dst, t0, *(dot(spreads(row, col), inputs) for row, col, inputs in (first, second)))

    def form_train(g):
        for half in (0, 1):
            ot[half] = tf[g, T_IN + 128 * half : T_IN + 128 * (half + 1), :].astype(F32).T
        for h in (0, 1):
            form(
                tmat,
                pl.multiple_of(g * 32 + 16 * h, 16),
                (64 * h, 0, tf[g, 256 * h : 256 * h + 128, :]),
                (64 * h, 1, tf[g, 256 * h + 128 : 256 * h + 256, :]),
            )

    def form_trains(low, high):
        def one(u):
            k, own = u // 2, u % 2
            core = jnp.where(own == 0, c, 1 - c)

            @pl.when(own == 1)
            def _():
                across(k, 1 - c).wait_recv()

            form_train(owner(k) * 2 + core)

        loop(low, high, one)

    for step in range(far):
        low, high = (0, 2) if step == 0 else (4 * step - 2, 4 * step + 2)
        lax.fori_loop(low, high, project, 0)
        for k in range(low // 2, high // 2):
            to_sibling(k, 0).wait_recv()
            to_sibling(k, 1).wait_recv()
        if step:
            short(step, 0)
        long(step, 0)
    long(0, 1)
    short(1, 1)
    lax.fori_loop(2 * nz - 2, 2 * nz, project, 0)
    to_sibling(nz - 1, 0).wait_recv()
    to_sibling(nz - 1, 1).wait_recv()

    def put_train(rows, value):
        tf[p, rows, :] = value

    def put_query(rows, value):
        qf[e, rows, :] = value

    final(0, put_train)

    def gram_local():
        t_in = tf[p, 0:T_IN, :]
        t_out = tf[p, T_IN:T_ALL, :]
        gi = dot(t_in, t_in, TN)
        go = dot(t_out, t_out, TN)
        gram_out = go[0:64, 0:64] + go[64:128, 64:128]
        gl[0:64, :] = gi[0:64, :]
        gl[64:128, :] = jnp.concatenate([gram_out, gi[64:128, 64:128]], axis=1)

    gram_local()
    loop(1, ne, lambda o: plane(0, part_for(o), g1, o).start())
    g1[e] = gl[pl.ds(pl.multiple_of(e * piece, piece), piece), :]
    long(1, 1)
    form_trains(0, 1)
    loop(1, ne, lambda o: plane_from(0, gl.at[pl.ds(0, piece)], g1, o).wait_recv())
    s1[...] = total(g1, ne)
    loop(1, np_, lambda o: column(o).start())
    g2[p] = s1[...]
    short(2, 1)
    long(2, 1)
    for way in (0, 1):
        pass_on(way, 0).start()
    across(0, c).start()
    loop(1, np_, lambda o: column_from(o).wait_recv())
    s2[...] = total(g2, np_)
    loop(1, ne, lambda o: plane(2, s2, g3, o).start())
    g3[e] = s2[...]
    for step in range(3, far):
        short(step, 1)
        long(step, 1)
    form_trains(1, 2)
    loop(1, ne, lambda o: plane_from(2, s2, g3, o).wait_recv())
    relay(1)
    gram = jnp.concatenate([g3[i] for i in range(ne)], axis=0)
    upper = gram[0:64, 64:128]
    gram_in = jnp.concatenate(
        [gram[0:64, :], jnp.concatenate([upper.T, gram[64:128, 64:128]], axis=1)], axis=0
    )
    inv_in = inverse_of(gram_in, count)
    inv_out = inverse_of(gram[64:128, 0:64], count)
    zero = jnp.zeros((64, 64), F32)
    both = jnp.concatenate(
        [jnp.concatenate([inv_out, zero], axis=1), jnp.concatenate([zero, inv_out], axis=1)], axis=0
    )

    final(1, put_query)
    q_start(0, 2)
    form_trains(2, 6)
    q_wait(0)
    q_start(1, 3, 4)
    relay(2)
    q_wait(1)
    q_start(5)
    form_trains(6, 10)
    for o, way in both_ways:
        for index in (0, 1):
            q_copy(o, way, 2 + 2 * way + index, False).wait_recv()
            q_copy(o, way, 6 + index, True).start()
    for step in range(3, far + 1):
        relay(step)
    form_trains(10, 2 * nz)

    def thirds(x):
        high = x.astype(BF16)
        mid, low = split(x - high.astype(F32))
        return high, mid, low

    in_parts, out_parts = thirds(inv_in), thirds(both)

    def apply(a, parts):
        return dot(a, parts[0]) + (dot(a, parts[1]) + dot(a, parts[2]))

    def form_query(i):
        side = apply(qf[i, Q_IN:Q_ALL, :], out_parts).T
        side_high = side.astype(BF16).astype(F32)
        ot[0] = side_high
        ot[1] = side - side_high
        high, low = split(apply(qf[i, 0:Q_IN, :], in_parts))
        wide = jnp.concatenate([high, low], axis=1)

        def product(h):
            rows = slice(128 * h, 128 * h + 128)
            main = dot(spreads(64 * h, 0), wide[rows])
            return main[:, 0:128] + (main[:, 128:256] + dot(spreads(64 * h, 1), high[rows]))

        put(qmat, pl.multiple_of(i * 16, 16), product(0), product(1))

    for o, way in both_ways:
        for slot in (4 - 2 * way, 5 - 2 * way, 6, 7):
            q_copy(o, way, slot, False).wait_recv()
    loop(0, ne, form_query)

    deep = 1024
    raw[...] = jnp.zeros_like(raw)

    def contract(i):
        at = pl.ds(pl.multiple_of(i * deep, deep), deep)
        raw[...] += dot(tmat[:, at], qmat[:, at], NT)

    loop(0, tmat.shape[1] // deep, contract)
    block = raw[...] * scale * allow[...]
    scores[...] = block
    high, low = split(block)
    hot = hot_t.astype(BF16)
    partial = (dot(hot, high) + dot(hot, low)) * spread
    share = partial.T.astype(BF16)
    rows = share.shape[0] // ne
    for i in range(ne):
        cs[i] = share[i * rows : (i + 1) * rows, :]

    def c_to(o):
        other = lax.rem(e + o, ne)
        return remote(cs.at[other], cr.at[e], c_send.at[o], c_recv.at[e], spot(p, other))

    def c_from(o):
        other = lax.rem(e + ne - o, ne)
        return remote(cs.at[other], cr.at[other], c_send.at[o], c_recv.at[other], spot(p, other))

    loop(1, ne, lambda o: c_to(o).start())
    cr[e] = cs[e]
    loop(1, ne, lambda o: c_from(o).wait_recv())
    acc = cr[0].astype(F32)
    for i in range(1, ne):
        acc = acc + cr[i].astype(F32)
    sums[...] = acc

    def drain(o):
        plane(0, part_for(o), g1, o).wait_send()
        plane(2, s2, g3, o).wait_send()
        c_to(o).wait_send()

    loop(1, ne, drain)
    for o, way in both_ways:
        for slot in range(8):
            q_copy(o, way, slot, True).wait_send()
    loop(1, np_, lambda o: column(o).wait_send())
    for step in range(far):
        for way in (0, 1):
            pass_on(way, step).wait_send()
    loop(0, nz, lambda k: across(k, c).wait_send())
    for copy in hops:
        copy.wait_send()
    for k in range(nz):
        to_sibling(k, 0).wait_send()
        to_sibling(k, 1).wait_send()


def solution(mesh):
    np_, ne = mesh.shape["param"], mesh.shape["ex"]
    nz = np_ // 2
    far = nz // 2

    def step(qa, qg, ta, tg, win, wout, query_clusters, train_clusters, pair_mask):
        groups, q_rows, tokens, feats = qa.shape
        t_rows = ta.shape[1]
        flat = [x.reshape(x.shape[0], x.shape[1] * x.shape[2], x.shape[3]) for x in (qa, qg, ta, tg)]
        any_space = pl.BlockSpec(memory_space=pl.ANY)
        vmem = pl.BlockSpec(memory_space=pltpu.VMEM)
        dma = pltpu.SemaphoreType.DMA
        limit = 63_000_000
        all_t, all_q = groups * t_rows, q_rows * ne
        dims = win.shape[1] * wout.shape[1]
        clusters = pair_mask.shape[0]
        total = groups * t_rows * ne
        scores, sums = pl.pallas_call(
            functools.partial(
                kernel,
                nz,
                ne,
                float(total * tokens),
                1.0 / (tokens * math.sqrt(dims)),
                math.sqrt(clusters / total),
            ),
            out_shape=(
                jax.ShapeDtypeStruct((all_t, all_q), F32),
                jax.ShapeDtypeStruct((q_rows, clusters), F32),
            ),
            in_specs=[any_space] * 4 + [vmem] * 5,
            out_specs=(vmem, vmem),
            scratch_shapes=[
                pltpu.VMEM((groups,) + flat[0].shape[1:], BF16),
                pltpu.VMEM((groups,) + flat[1].shape[1:], BF16),
                pltpu.VMEM((groups,) + flat[2].shape[1:], BF16),
                pltpu.VMEM((groups,) + flat[3].shape[1:], BF16),
                pltpu.VMEM((2, nz, T_ALL, 128), BF16),
                pltpu.VMEM((2, nz, Q_ALL, 128), F32),
                pltpu.VMEM((nz, T_ALL, 128), BF16),
                pltpu.VMEM((nz, Q_ALL, 128), F32),
                pltpu.VMEM((2, far, T_ALL, 128), BF16),
                pltpu.VMEM((2, far, Q_ALL, 128), F32),
                pltpu.VMEM((2, far, T_ALL, 128), BF16),
                pltpu.VMEM((2, far, Q_ALL, 128), F32),
                pltpu.VMEM((groups, T_ALL, 128), BF16),
                pltpu.VMEM((ne, Q_ALL, 128), BF16),
                pltpu.VMEM((128, 128), F32),
                pltpu.VMEM((ne, 128 // ne, 128), F32),
                pltpu.VMEM((np_, 128 // ne, 128), F32),
                pltpu.VMEM((ne, 128 // ne, 128), F32),
                pltpu.VMEM((128 // ne, 128), F32),
                pltpu.VMEM((128 // ne, 128), F32),
                pltpu.VMEM((all_t, dims), BF16),
                pltpu.VMEM((all_q, dims), BF16),
                pltpu.VMEM((2, 128, 128), F32),
                pltpu.VMEM((all_t, all_q), F32),
                pltpu.VMEM((all_t, all_q), F32),
                pltpu.VMEM((ne, q_rows, clusters), BF16),
                pltpu.VMEM((ne, q_rows, clusters), BF16),
                dma((4, groups)),
                dma((2, nz)),
                dma((2, nz)),
                dma((2, far, 2, 2)),
                dma((2, far, 2, 2)),
                dma((3, max(ne, np_))),
                dma((3, max(ne, np_))),
                dma((2, 2, 8)),
                dma((2, 2, 8)),
                dma((2, far)),
                dma((2, far)),
                dma((nz,)),
                dma((nz,)),
                dma((ne,)),
                dma((ne,)),
            ],
            compiler_params=pltpu.CompilerParams(
                collective_id=0, has_side_effects=True, vmem_limit_bytes=limit
            ),
            name="score",
        )(*flat, win, wout.T, query_clusters, train_clusters.reshape(1, -1), pair_mask)
        return (
            scores.T.reshape(1, all_q, groups, t_rows),
            sums.reshape(1, q_rows, clusters),
        )

    return jax.shard_map(
        step,
        mesh=mesh,
        in_specs=(
            P(None, "ex", None, "param"),
            P(None, "ex", None, "param"),
            P(None, "ex", None, "param"),
            P(None, "ex", None, "param"),
            P("param", None),
            P("param", None),
            P("param", None),
            P(None, "ex"),
            P(),
        ),
        out_specs=(P("param", None, None, "ex"), P("param", "ex", None)),
        check_vma=False,
    )
```

```python
import functools
import math

import jax
import jax.numpy as jnp
from jax import lax
from jax.experimental import pallas as pl
from jax.experimental.pallas import tpu as pltpu
from jax.sharding import PartitionSpec as P

MESH = pl.DeviceIdType.MESH
F32 = jnp.float32
BF16 = jnp.bfloat16
NT = (((1,), (1,)), ((), ()))
TN = (((0,), (0,)), ((), ()))

T_IN, T_ALL = 512, 768
Q_IN, ALL = 256, 1152
Q_ALL = ALL - T_ALL


def remote(src, dst, send, recv, device):
    return pltpu.make_async_remote_copy(
        src_ref=src, dst_ref=dst, send_sem=send, recv_sem=recv, device_id=device, device_id_type=MESH
    )


def spot(p, e):
    return {"param": p, "ex": e}


def halves(chunk):
    size = (T_ALL, Q_ALL)[chunk] // 2
    return (pl.ds(0, size), pl.ds(size, size))


def newton(damped, level, steps, scalings):
    size = damped.shape[0]
    rows = lax.broadcasted_iota(jnp.int32, (size, size), 0)
    eye = (rows == lax.broadcasted_iota(jnp.int32, (size, size), 1)).astype(F32)

    def dot(a, b):
        return jnp.dot(a, b, preferred_element_type=F32, precision=lax.Precision.HIGHEST)

    resid = eye - level * damped
    guess = level * eye
    for index in range(steps):
        c = scalings[index]
        grown = guess + (level * resid if index == 0 else dot(guess, resid))
        resid = (1.0 - c) * eye + c * dot(resid, resid)
        guess = c * grown
    for _ in range(2):
        resid = eye - dot(damped, guess)
        guess = guess + dot(guess, resid)
    return 0.5 * (guess + guess.T)


def schedule_of(size):
    kappa = 1.0 + 10.0 * size
    rho = (kappa - 1.0) / (kappa + 1.0)
    scalings = []
    while rho > 1e-4:
        scalings.append(2.0 / (2.0 - rho * rho))
        rho = rho * rho / (2.0 - rho * rho)
    return 2.0 / (1.0 + kappa), scalings


def inverse_of(gram, count):
    size = gram.shape[0]
    mean = gram * (1.0 / count)
    rows = lax.broadcasted_iota(jnp.int32, (size, size), 0)
    diagonal = rows == lax.broadcasted_iota(jnp.int32, (size, size), 1)
    floor = 0.1 / size * jnp.sum(jnp.where(diagonal, mean, 0.0), keepdims=True)
    damped = mean + jnp.where(diagonal, floor, 0.0)
    level, scalings = schedule_of(size)
    return newton(damped, level / floor, len(scalings), scalings)


def kernel(
    nz, ne, count, scale, spread,
    qa, qg, ta, tg, win, wout, query_ids, train_ids, mask,
    scores, sums,
    qa_b, qg_b, ta_b, tg_b, part_t, part_q, sib_t, sib_q, snd_t, snd_q, rcv_t, rcv_q,
    tf, qf, gl, g1, g2, g3, s1, s2, tmat, qmat, ot, raw, allow, cs, cr,
    in_sem, sib_send, sib_recv, ring_send, ring_recv,
    g_send, g_recv, q_send, q_recv, t_send, t_recv, over_send, over_recv, c_send, c_recv,
):
    p, e = lax.axis_index("param"), lax.axis_index("ex")
    np_ = 2 * nz
    z, c = p // 2, p % 2
    sibling = spot(z * 2 + 1 - c, e)
    ring = (spot(lax.rem(z + 1, nz) * 2 + c, e), spot(lax.rem(z + nz - 1, nz) * 2 + c, e))
    far = nz // 2

    def shift(k):
        m = far - (k + 1) // 2
        return jnp.where(k % 2 == 1, m, nz - m) % nz

    def group(u):
        k = u // 2
        core = jnp.where(u % 2 == 0, 1 - c, c)
        return lax.rem(z + shift(k), nz) * 2 + core

    pairs = (((ta, ta_b), (tg, tg_b)), ((qa, qa_b), (qg, qg_b)))

    def loads(u, chunk):
        g = group(u)
        return [
            pltpu.make_async_copy(src.at[g], dst.at[u], in_sem.at[2 * chunk + i, u])
            for i, (src, dst) in enumerate(pairs[chunk])
        ]

    for chunk in (0, 1):

        def start(u, carry):
            for copy in loads(u, chunk):
                copy.start()
            return carry

        lax.fori_loop(0, 2 * nz, start, 0)

    barrier = pltpu.get_barrier_semaphore()

    def greet(o, carry):
        pl.semaphore_signal(barrier, inc=1, device_id=spot(p, lax.rem(e + o, ne)), device_id_type=MESH)
        return carry

    def greet_column(o, carry):
        pl.semaphore_signal(barrier, inc=1, device_id=spot(lax.rem(p + o, np_), e), device_id_type=MESH)
        return carry

    lax.fori_loop(1, ne, greet, 0)
    lax.fori_loop(1, np_, greet_column, 0)

    def dot(a, b, dims=None):
        if dims is None:
            return jnp.dot(a, b, preferred_element_type=F32)
        return lax.dot_general(a, b, dims, preferred_element_type=F32)

    width = mask.shape[0]
    cluster_q = lax.broadcasted_iota(jnp.int32, (width, query_ids.shape[1]), 0)
    hot_q = jnp.where(cluster_q == query_ids[...], 1.0, 0.0)
    ids = jnp.concatenate([train_ids[g : g + 1, :] for g in range(train_ids.shape[0])], axis=1)
    cluster_t = lax.broadcasted_iota(jnp.int32, (width, ids.shape[1]), 0)
    hot_t = jnp.where(cluster_t == ids, 1.0, 0.0)
    picked = dot(mask[...].astype(F32).T.astype(BF16), hot_q.astype(BF16))
    allow[...] = dot(hot_t.T.astype(BF16), picked.astype(BF16))

    pl.semaphore_wait(barrier, ne + np_ - 2)

    w_in = win[...]
    narrow = wout[...].astype(F32).T
    blank = jnp.zeros_like(narrow)
    w_low = jnp.concatenate([narrow, blank], axis=1).astype(BF16)
    w_high = jnp.concatenate([blank, narrow], axis=1).astype(BF16)

    parts, sibs, sends, recvs = (part_t, part_q), (sib_t, sib_q), (snd_t, snd_q), (rcv_t, rcv_q)

    def to_sibling(k, chunk):
        return remote(
            parts[chunk].at[0, k], sibs[chunk].at[k], sib_send.at[chunk, k], sib_recv.at[chunk, k], sibling
        )

    def project_train(u):
        for copy in loads(u, 0):
            copy.wait()
        k, own = u // 2, u % 2
        part_t[own, k, 0:T_IN, :] = dot(ta_b[u], w_in).astype(BF16)
        part_t[own, k, T_IN:T_ALL, :] = (
            dot(tg_b[u, 0:256, :], w_low) + dot(tg_b[u, 256:512, :], w_high)
        ).astype(BF16)

        @pl.when(own == 0)
        def _():
            to_sibling(k, 0).start()

    def project_query(u):
        for copy in loads(u, 1):
            copy.wait()
        k, own = u // 2, u % 2
        part_q[own, k, 0:Q_IN, :] = dot(qa_b[u], w_in)
        part_q[own, k, Q_IN:Q_ALL, :] = dot(qg_b[u, 0:128, :], w_low) + dot(qg_b[u, 128:256, :], w_high)

        @pl.when(own == 0)
        def _():
            to_sibling(k, 1).start()

    def hop(way, step, chunk, half):
        rows = halves(chunk)[half]
        return remote(
            sends[chunk].at[way, step, rows],
            recvs[chunk].at[way, step, rows],
            ring_send.at[way, step, chunk, half],
            ring_recv.at[way, step, chunk, half],
            ring[way],
        )

    def own_sum(k, chunk, rows):
        return parts[chunk][1, k, rows, :].astype(F32) + sibs[chunk][k, rows, :].astype(F32)

    hops = []

    def send(way, step, chunk, half):
        rows = halves(chunk)[half]
        k = 0 if step == 0 else 2 * step - 1 + way
        value = own_sum(k, chunk, rows)
        if step >= 2 or (step == 1 and half == way):
            hop(way, step - 1, chunk, half).wait_recv()
            value = value + recvs[chunk][way, step - 1, rows, :].astype(F32)
        sends[chunk][way, step, rows, :] = value.astype(sends[chunk].dtype)
        copy = hop(way, step, chunk, half)
        copy.start()
        hops.append(copy)

    def short(step, chunk):
        for way in (0, 1):
            send(way, step, chunk, 1 - way)

    def long(step, chunk):
        for way in (0, 1):
            send(way, step, chunk, way)

    def final(chunk, put):
        for index in (1, 0):
            rows = halves(chunk)[index]
            value = own_sum(nz - 1, chunk, rows)
            for way in (0, 1):
                hop(way, far - 1, chunk, index).wait_recv()
                value = value + recvs[chunk][way, far - 1, rows, :].astype(F32)
            put(rows, value.astype(BF16))

    piece = gl.shape[0] // ne

    def plane(phase, src, dst, o):
        return remote(
            src, dst.at[e], g_send.at[phase, o], g_recv.at[phase, e], spot(p, lax.rem(e + o, ne))
        )

    def plane_from(phase, src, dst, o):
        other = lax.rem(e + ne - o, ne)
        return remote(src, dst.at[other], g_send.at[phase, o], g_recv.at[phase, other], spot(p, other))

    def column(o):
        return remote(s1, g2.at[p], g_send.at[1, o], g_recv.at[1, p], spot(lax.rem(p + o, np_), e))

    def column_from(o):
        other = lax.rem(p + np_ - o, np_)
        return remote(s1, g2.at[other], g_send.at[1, o], g_recv.at[1, other], spot(other, e))

    def part_for(o):
        start = pl.multiple_of(lax.rem(e + o, ne) * piece, piece)
        return gl.at[pl.ds(start, piece)]

    def loop(low, high, body):
        def step(i, carry):
            body(i)
            return carry

        lax.fori_loop(low, high, step, 0)

    rows_of = (pl.ds(0, T_ALL // 2), pl.ds(T_ALL // 2, T_ALL // 2))

    def owner(k):
        s = (k + 1) // 2
        return lax.rem(z + jnp.where(k % 2 == 1, nz - s, s), nz)

    def pass_on(way, step):
        s = step if way == 1 else nz - step
        block = lax.rem(z + s, nz) * 2 + c
        ref = tf.at[block] if step < far - 1 else tf.at[block, rows_of[way]]
        return remote(ref, ref, t_send.at[way, step], t_recv.at[way, step], ring[way])

    def arrival(way, step):
        s = step + 1 if way == 1 else nz - step - 1
        block = lax.rem(z + s, nz) * 2 + c
        ref = tf.at[block] if step < far - 1 else tf.at[block, rows_of[way]]
        return remote(ref, ref, t_send.at[way, step], t_recv.at[way, step], ring[way])

    def across(k, core):
        ref = tf.at[owner(k) * 2 + core]
        return remote(ref, ref, over_send.at[k], over_recv.at[k], sibling)

    edge = math.isqrt(ne)
    half = Q_ALL // 2

    def place(o, da, db):
        a, b = (e // edge, e % edge) if o == 0 else (e % edge, e // edge)
        a, b = lax.rem(a + da + edge, edge), lax.rem(b + db + edge, edge)
        return a * edge + b if o == 0 else b * edge + a

    along = (0, -1, 1, 2)

    def q_copy(o, way, slot, sending):
        back = 0 if sending else (-1 if way == 0 else 1)
        sign = 1 if way == 0 else -1
        rows = pl.ds(half * o, half)
        if slot == 0:
            block, target = place(o, back, 0), place(o, sign, 0)
        elif slot == 1:
            block, target = place(o, back - sign, 0), place(o, sign, 0)
            rows = pl.ds(half * o + half // 2 * way, half // 2)
        elif slot < 6:
            block, target = place(o, along[slot - 2], back), place(o, 0, sign)
        else:
            block, target = place(o, along[2 * way + slot - 6], back - sign), place(o, 0, sign)
        ref = qf.at[block, rows]
        return remote(ref, ref, q_send.at[o, way, slot], q_recv.at[o, way, slot], spot(p, target))

    both_ways = [(o, way) for o in (0, 1) for way in (0, 1)]

    def q_start(*slots):
        for slot in slots:
            for o, way in both_ways:
                q_copy(o, way, slot, True).start()

    def q_wait(*slots):
        for slot in slots:
            for o, way in both_ways:
                q_copy(o, way, slot, False).wait_recv()

    def total(ref, n):
        value = ref[0]
        for i in range(1, n):
            value = value + ref[i]
        return value

    def relay(step):
        for way in (0, 1):
            arrival(way, step - 1).wait_recv()
            if step < far:
                pass_on(way, step).start()
                across(2 * step - 1 + way, c).start()
        if step == far:
            across(nz - 1, c).start()

    def split(x):
        high = x.astype(BF16)
        return high, (x - high.astype(F32)).astype(BF16)

    lane = lax.broadcasted_iota(jnp.int32, (8, 128), 1) // 16
    own_tokens = jnp.where(lane == lax.broadcasted_iota(jnp.int32, (8, 128), 0), 1.0, 0.0)

    def spreads(row, col):
        rows = [ot[col, pl.ds(row + r, 8, stride=0), :] * own_tokens for r in range(64)]
        return jnp.concatenate(rows, axis=0).astype(BF16)

    def put(dst, t0, a, b):
        for r in range(64):
            tile = jnp.concatenate([a[8 * r : 8 * r + 8], b[8 * r : 8 * r + 8]], axis=0)
            dst[pl.ds(t0, 16), 128 * r : 128 * (r + 1)] = tile.astype(BF16)

    def form(dst, t0, first, second):
        put(dst, t0, *(dot(spreads(row, col), inputs) for row, col, inputs in (first, second)))

    def form_train(g):
        for half in (0, 1):
            ot[half] = tf[g, T_IN + 128 * half : T_IN + 128 * (half + 1), :].astype(F32).T
        for h in (0, 1):
            form(
                tmat,
                pl.multiple_of(g * 32 + 16 * h, 16),
                (64 * h, 0, tf[g, 256 * h : 256 * h + 128, :]),
                (64 * h, 1, tf[g, 256 * h + 128 : 256 * h + 256, :]),
            )

    def form_trains(low, high):
        def one(u):
            k, own = u // 2, u % 2
            core = jnp.where(own == 0, c, 1 - c)

            @pl.when(own == 1)
            def _():
                across(k, 1 - c).wait_recv()

            form_train(owner(k) * 2 + core)

        loop(low, high, one)

    def sibling_sent(low, high, chunk):
        for k in range(low, high):
            to_sibling(k, chunk).wait_recv()

    for step in range(far):
        low, high = (0, 1) if step == 0 else (2 * step - 1, 2 * step + 1)
        loop(2 * low, 2 * high, project_train)
        sibling_sent(low, high, 0)
        if step:
            short(step, 0)
        long(step, 0)
    loop(0, 6, project_query)
    sibling_sent(0, 1, 1)
    long(0, 1)
    loop(2 * nz - 2, 2 * nz, project_train)
    sibling_sent(1, 3, 1)
    short(1, 1)
    loop(6, 2 * nz, project_query)
    sibling_sent(nz - 1, nz, 0)

    def put_train(rows, value):
        tf[p, rows, :] = value

    def put_query(rows, value):
        qf[e, rows, :] = value

    final(0, put_train)

    def gram_local():
        t_in = tf[p, 0:T_IN, :]
        t_out = tf[p, T_IN:T_ALL, :]
        gi = dot(t_in, t_in, TN)
        go = dot(t_out, t_out, TN)
        gram_out = go[0:64, 0:64] + go[64:128, 64:128]
        gl[0:64, :] = gi[0:64, :]
        gl[64:128, :] = jnp.concatenate([gram_out, gi[64:128, 64:128]], axis=1)

    gram_local()
    loop(1, ne, lambda o: plane(0, part_for(o), g1, o).start())
    g1[e] = gl[pl.ds(pl.multiple_of(e * piece, piece), piece), :]
    long(1, 1)
    form_trains(0, 1)
    loop(1, ne, lambda o: plane_from(0, gl.at[pl.ds(0, piece)], g1, o).wait_recv())
    s1[...] = total(g1, ne)
    loop(1, np_, lambda o: column(o).start())
    g2[p] = s1[...]
    sibling_sent(3, nz, 1)
    short(2, 1)
    long(2, 1)
    for way in (0, 1):
        pass_on(way, 0).start()
    across(0, c).start()
    loop(1, np_, lambda o: column_from(o).wait_recv())
    s2[...] = total(g2, np_)
    loop(1, ne, lambda o: plane(2, s2, g3, o).start())
    g3[e] = s2[...]
    for step in range(3, far):
        short(step, 1)
        long(step, 1)
    form_trains(1, 2)
    loop(1, ne, lambda o: plane_from(2, s2, g3, o).wait_recv())
    relay(1)
    gram = jnp.concatenate([g3[i] for i in range(ne)], axis=0)
    upper = gram[0:64, 64:128]
    gram_in = jnp.concatenate(
        [gram[0:64, :], jnp.concatenate([upper.T, gram[64:128, 64:128]], axis=1)], axis=0
    )
    inv_in = inverse_of(gram_in, count)
    inv_out = inverse_of(gram[64:128, 0:64], count)
    zero = jnp.zeros((64, 64), F32)
    both = jnp.concatenate(
        [jnp.concatenate([inv_out, zero], axis=1), jnp.concatenate([zero, inv_out], axis=1)], axis=0
    )

    def thirds(x):
        high = x.astype(BF16)
        mid, low = split(x - high.astype(F32))
        return high, mid, low

    in_parts, out_parts = thirds(inv_in), thirds(both)

    def apply(a, parts):
        return dot(a, parts[0]) + (dot(a, parts[1]) + dot(a, parts[2]))

    def form_query(i):
        side = apply(qf[i, Q_IN:Q_ALL, :], out_parts).T
        side_high = side.astype(BF16).astype(F32)
        ot[0] = side_high
        ot[1] = side - side_high
        high, low = split(apply(qf[i, 0:Q_IN, :], in_parts))
        wide = jnp.concatenate([high, low], axis=1)

        def product(h):
            rows = slice(128 * h, 128 * h + 128)
            main = dot(spreads(64 * h, 0), wide[rows])
            return main[:, 0:128] + (main[:, 128:256] + dot(spreads(64 * h, 1), high[rows]))

        put(qmat, pl.multiple_of(i * 16, 16), product(0), product(1))

    final(1, put_query)
    q_start(0, 2)
    form_trains(2, 6)
    q_wait(0)
    q_start(1, 3, 4)
    q_wait(1)
    q_start(5)
    form_query(e)
    relay(2)
    q_wait(2)

    def near(i):
        step = 2 * (i % 2) - 1
        form_query(place(0, jnp.where(i < 2, step, 0), jnp.where(i < 2, 0, step)))

    loop(0, 4, near)
    q_wait(3, 4)
    for o, way in both_ways:
        for index in (0, 1):
            if way and index:
                q_copy(o, way, 5, False).wait_recv()
            q_copy(o, way, 6 + index, True).start()

    def corner(i):
        form_query(place(0, 2 * (i % 2) - 1, 2 * (i // 2) - 1))

    loop(0, 4, corner)
    for step in range(3, far):
        relay(step)
    form_trains(6, 10)
    relay(far)
    form_trains(10, 2 * nz)

    for o in (0, 1):
        q_copy(o, 0, 5, False).wait_recv()
    q_wait(6, 7)

    def distant(i):
        form_query(place(0, jnp.where(i < 4, 2, i - 5), jnp.where(i < 4, i - 1, 2)))

    loop(0, 7, distant)

    deep = 2048
    raw[...] = jnp.zeros_like(raw)

    def contract(i):
        at = pl.ds(pl.multiple_of(i * deep, deep), deep)
        raw[...] += dot(tmat[:, at], qmat[:, at], NT)

    loop(0, tmat.shape[1] // deep, contract)
    block = raw[...] * scale * allow[...]
    scores[...] = block
    high, low = split(block)
    hot = hot_t.astype(BF16)
    partial = (dot(hot, high) + dot(hot, low)) * spread
    share = partial.T.astype(BF16)
    rows = share.shape[0] // ne
    for i in range(ne):
        cs[i] = share[i * rows : (i + 1) * rows, :]

    def c_to(o):
        other = lax.rem(e + o, ne)
        return remote(cs.at[other], cr.at[e], c_send.at[o], c_recv.at[e], spot(p, other))

    def c_from(o):
        other = lax.rem(e + ne - o, ne)
        return remote(cs.at[other], cr.at[other], c_send.at[o], c_recv.at[other], spot(p, other))

    loop(1, ne, lambda o: c_to(o).start())
    cr[e] = cs[e]
    loop(1, ne, lambda o: c_from(o).wait_recv())
    acc = cr[0].astype(F32)
    for i in range(1, ne):
        acc = acc + cr[i].astype(F32)
    sums[...] = acc

    def drain(o):
        plane(0, part_for(o), g1, o).wait_send()
        plane(2, s2, g3, o).wait_send()
        c_to(o).wait_send()

    loop(1, ne, drain)
    for o, way in both_ways:
        for slot in range(8):
            q_copy(o, way, slot, True).wait_send()
    loop(1, np_, lambda o: column(o).wait_send())
    for step in range(far):
        for way in (0, 1):
            pass_on(way, step).wait_send()
    loop(0, nz, lambda k: across(k, c).wait_send())
    for copy in hops:
        copy.wait_send()
    for k in range(nz):
        to_sibling(k, 0).wait_send()
        to_sibling(k, 1).wait_send()


def solution(mesh):
    np_, ne = mesh.shape["param"], mesh.shape["ex"]
    nz = np_ // 2
    far = nz // 2

    def step(qa, qg, ta, tg, win, wout, query_clusters, train_clusters, pair_mask):
        groups, q_rows, tokens, feats = qa.shape
        t_rows = ta.shape[1]
        flat = [x.reshape(x.shape[0], x.shape[1] * x.shape[2], x.shape[3]) for x in (qa, qg, ta, tg)]
        any_space = pl.BlockSpec(memory_space=pl.ANY)
        vmem = pl.BlockSpec(memory_space=pltpu.VMEM)
        dma = pltpu.SemaphoreType.DMA
        limit = 63_000_000
        all_t, all_q = groups * t_rows, q_rows * ne
        dims = win.shape[1] * wout.shape[1]
        clusters = pair_mask.shape[0]
        total = groups * t_rows * ne
        scores, sums = pl.pallas_call(
            functools.partial(
                kernel,
                nz,
                ne,
                float(total * tokens),
                1.0 / (tokens * math.sqrt(dims)),
                math.sqrt(clusters / total),
            ),
            out_shape=(
                jax.ShapeDtypeStruct((all_t, all_q), F32),
                jax.ShapeDtypeStruct((q_rows, clusters), F32),
            ),
            in_specs=[any_space] * 4 + [vmem] * 5,
            out_specs=(vmem, vmem),
            scratch_shapes=[
                pltpu.VMEM((groups,) + flat[0].shape[1:], BF16),
                pltpu.VMEM((groups,) + flat[1].shape[1:], BF16),
                pltpu.VMEM((groups,) + flat[2].shape[1:], BF16),
                pltpu.VMEM((groups,) + flat[3].shape[1:], BF16),
                pltpu.VMEM((2, nz, T_ALL, 128), BF16),
                pltpu.VMEM((2, nz, Q_ALL, 128), F32),
                pltpu.VMEM((nz, T_ALL, 128), BF16),
                pltpu.VMEM((nz, Q_ALL, 128), F32),
                pltpu.VMEM((2, far, T_ALL, 128), BF16),
                pltpu.VMEM((2, far, Q_ALL, 128), F32),
                pltpu.VMEM((2, far, T_ALL, 128), BF16),
                pltpu.VMEM((2, far, Q_ALL, 128), F32),
                pltpu.VMEM((groups, T_ALL, 128), BF16),
                pltpu.VMEM((ne, Q_ALL, 128), BF16),
                pltpu.VMEM((128, 128), F32),
                pltpu.VMEM((ne, 128 // ne, 128), F32),
                pltpu.VMEM((np_, 128 // ne, 128), F32),
                pltpu.VMEM((ne, 128 // ne, 128), F32),
                pltpu.VMEM((128 // ne, 128), F32),
                pltpu.VMEM((128 // ne, 128), F32),
                pltpu.VMEM((all_t, dims), BF16),
                pltpu.VMEM((all_q, dims), BF16),
                pltpu.VMEM((2, 128, 128), F32),
                pltpu.VMEM((all_t, all_q), F32),
                pltpu.VMEM((all_t, all_q), F32),
                pltpu.VMEM((ne, q_rows, clusters), BF16),
                pltpu.VMEM((ne, q_rows, clusters), BF16),
                dma((4, groups)),
                dma((2, nz)),
                dma((2, nz)),
                dma((2, far, 2, 2)),
                dma((2, far, 2, 2)),
                dma((3, max(ne, np_))),
                dma((3, max(ne, np_))),
                dma((2, 2, 8)),
                dma((2, 2, 8)),
                dma((2, far)),
                dma((2, far)),
                dma((nz,)),
                dma((nz,)),
                dma((ne,)),
                dma((ne,)),
            ],
            compiler_params=pltpu.CompilerParams(
                collective_id=0, has_side_effects=True, vmem_limit_bytes=limit
            ),
            name="score",
        )(*flat, win, wout.T, query_clusters, train_clusters, pair_mask)
        return (
            scores.T.reshape(1, all_q, groups, t_rows),
            sums.reshape(1, q_rows, clusters),
        )

    return jax.shard_map(
        step,
        mesh=mesh,
        in_specs=(
            P(None, "ex", None, "param"),
            P(None, "ex", None, "param"),
            P(None, "ex", None, "param"),
            P(None, "ex", None, "param"),
            P("param", None),
            P("param", None),
            P("param", None),
            P(None, "ex"),
            P(),
        ),
        out_specs=(P("param", None, None, "ex"), P("param", "ex", None)),
        check_vma=False,
    )
```
